512 devices in a mesh: ctx: 64 (over y, z), head: 8 (over x, core).
Axes of the slice: x: 4, y: 4, z: 16, core: 2. Of those that a mesh axis runs over, the one named last changes fastest.
Arguments:
- queries: bfloat16 [32768, 2048], P('ctx', 'head'), may hold values from -16 to 16
- keys: bfloat16 [32768, 2048], P('ctx', 'head'), may hold values from -16 to 16
- values: bfloat16 [32768, 2048], P('ctx', 'head'), may hold values from -12 to 12
- gain: bfloat16 [2048], P('head'), may hold values from 0.5 to 1.5
- cotangent: bfloat16 [32768, 2048], P('ctx', 'head'), may hold values from -6 to 6
Outputs:
- output: bfloat16 [32768, 2048], P('ctx', 'head')
- grad_queries: bfloat16 [32768, 2048], P('ctx', 'head')
- grad_keys: bfloat16 [32768, 2048], P('ctx', 'head')
- grad_values: bfloat16 [32768, 2048], P('ctx', 'head')
The draws below stay inside these ranges and needn't reach their ends.
All inputs are finite; a program needn't handle non-finite values.
Results may differ from the reference program's by a relative error of at most 0.0065.
Values may be sent and summed in bfloat16 or wider, within the bound.
A program may use at most 64 MiB of HBM per device.

```python
import math
import jax
import jax.numpy as jnp
from jax import lax

HEAD_DIM = 128
HEADS = 16
WINDOW = 256
TOK_DEV = 512
TOKENS = 32768
FEATURES = 2048


def draw_queries(key, part):
    own_part = jnp.clip(jax.random.normal(jax.random.fold_in(key, 1), (TOKENS, FEATURES), jnp.float32), -5.0, 5.0)
    return own_part.astype(jnp.bfloat16)


def draw_keys(key, part):
    own_part = jnp.clip(jax.random.normal(jax.random.fold_in(key, 2), (TOKENS, FEATURES), jnp.float32), -5.0, 5.0)
    return own_part.astype(jnp.bfloat16)


def draw_values(key, part):
    key_entry, key_jitter = jax.random.split(jax.random.fold_in(key, 3), 2)
    grade = jnp.arange(HEADS, dtype=jnp.float32) / max(HEADS - 1, 1)
    jitter = jnp.exp(jax.random.uniform(key_jitter, (HEADS,), jnp.float32, -0.15, 0.15))
    head_scale = 0.5 * jnp.exp(grade * jnp.log(3.0)) * jitter
    entries = jnp.clip(jax.random.normal(key_entry, (TOKENS, HEADS, HEAD_DIM), jnp.float32), -6.0, 6.0)
    return (entries * head_scale[None, :, None]).reshape(TOKENS, FEATURES).astype(jnp.bfloat16)


def block_scale(stream_key, shape, pieces, smallest, high):
    def one(position, blocks):
        heights = jax.random.uniform(jax.random.fold_in(jax.random.fold_in(stream_key, 6), position), (blocks,), jnp.float32, smallest / len(pieces), high / len(pieces))
        return jnp.repeat(jnp.exp(heights), shape[position] // blocks).reshape((-1,) + (1,) * (len(shape) - position - 1))

    factor_of = one(*pieces[0])
    for cut in pieces[1:]:
        factor_of = factor_of * one(*cut)
    return factor_of


def bell_draw(key, shape, spread, limit, cuts=(), kind=jnp.bfloat16):
    result = spread * jax.random.normal(key, shape, jnp.float32)
    if cuts:
        result = result * block_scale(key, shape, cuts, -0.22, 0.18)
    return jnp.clip(result, -limit, limit).astype(kind)


def setup_inputs(seed: int = 0) -> dict:
    splits = jax.random.split(jax.random.key(seed), 6)
    return {
        "queries": draw_queries(jax.random.fold_in(splits[5], 71), 0),
        "keys": draw_keys(jax.random.fold_in(splits[5], 71), 0),
        "values": draw_values(jax.random.fold_in(splits[5], 71), 0),
        "gain": jnp.clip(1.0 + 0.1 * jax.random.normal(splits[3], (FEATURES,), jnp.float32), 0.5, 1.5).astype(jnp.bfloat16),
        "cotangent": bell_draw(splits[4], (TOKENS, FEATURES), 1.0, 6.0, ((0, 64), (1, 8))),
    }


epsilon = 1e-06

def matmul(left, right):
    return jnp.dot(left, right, preferred_element_type=jnp.float32)

def reference(queries, keys, values, gain, cotangent):
    seq_len = queries.shape[0]
    num_blocks = seq_len // TOK_DEV
    inv_root = 1.0 / math.sqrt(HEAD_DIM)

    def by_head(array):
        return array.reshape(num_blocks, TOK_DEV, HEADS, HEAD_DIM).transpose(2, 0, 1, 3)

    def from_heads(array):
        return array.transpose(1, 2, 0, 3).reshape(seq_len, FEATURES)
    positions = jnp.arange(seq_len, dtype=jnp.int32)
    coefs = 1.0 / jnp.sqrt(HEAD_DIM * (positions + 1).astype(jnp.float32))
    coef_blocks = coefs.reshape(num_blocks, TOK_DEV)
    in_block = jnp.arange(TOK_DEV, dtype=jnp.int32)
    causal = in_block[:, None] >= in_block[None, :]
    ext_cols = jnp.arange(TOK_DEV + WINDOW, dtype=jnp.int32)
    block_ids = jnp.arange(num_blocks, dtype=jnp.int32)

    def window_mask(block_id):
        after = ext_cols[None, :] > in_block[:, None]
        within = ext_cols[None, :] <= in_block[:, None] + WINDOW
        inside = block_id * TOK_DEV - WINDOW + ext_cols[None, :] >= 0
        return after & within & inside

    def with_tails(array_h):
        tails = array_h[:-1, TOK_DEV - WINDOW:]
        return jnp.concatenate([jnp.zeros((1, WINDOW, HEAD_DIM), array_h.dtype), tails], 0)

    def forward_head(operands):
        query_h, key_h, value_h = operands

        def step(state, inputs):
            query_blk, key_blk, value_blk, key_tail, value_tail, coef_row, block_id = inputs
            state_b = state.astype(jnp.bfloat16)
            lin_weights = jnp.where(causal, matmul(query_blk, key_blk.T) * coef_row[:, None], 0.0).astype(jnp.bfloat16)
            linear = coef_row[:, None] * matmul(query_blk, state_b) + matmul(lin_weights, value_blk)
            key_ext = jnp.concatenate([key_tail, key_blk], 0)
            value_ext = jnp.concatenate([value_tail, value_blk], 0)
            mask = window_mask(block_id)
            logits = matmul(query_blk, key_ext.T) * inv_root
            row_peak = lax.optimization_barrier(jnp.max(jnp.where(mask, logits, -1e+30), 1))
            row_total = lax.optimization_barrier(jnp.sum(jnp.where(mask, jnp.exp(logits - row_peak[:, None]), 0.0), 1))
            log_total = row_peak + jnp.log(row_total)
            probs = jnp.where(mask, jnp.exp(logits - log_total[:, None]), 0.0)
            local_window = matmul(probs.astype(jnp.bfloat16), value_ext)
            return (state + matmul(key_blk.T, value_blk), (linear + local_window, local_window, log_total, state_b))
        init = jnp.zeros((HEAD_DIM, HEAD_DIM), jnp.float32)
        _, results = lax.scan(step, init, (query_h, key_h, value_h, with_tails(key_h), with_tails(value_h), coef_blocks, block_ids))
        return results
    query_all, key_all, value_all = (by_head(queries), by_head(keys), by_head(values))
    hidden_h, window_h, lse_h, prefix_h = lax.map(forward_head, (query_all, key_all, value_all))
    hidden = from_heads(hidden_h)
    gain_f = gain.astype(jnp.float32)
    scaled = gain_f[None, :] * cotangent.astype(jnp.float32)
    squares = lax.optimization_barrier(jnp.sum(hidden * hidden, 1))
    crossed = lax.optimization_barrier(jnp.sum(hidden * scaled, 1))
    recip = 1.0 / jnp.sqrt(squares / FEATURES + epsilon)
    output = (hidden * recip[:, None] * gain_f[None, :]).astype(jnp.bfloat16)
    grad_full = recip[:, None] * scaled - hidden * (recip ** 3 * crossed / FEATURES)[:, None]
    grad_h = grad_full.astype(jnp.bfloat16)
    grad_u = (grad_full * coefs[:, None]).astype(jnp.bfloat16)

    def backward_head(operands):
        query_h, key_h, value_h, grad_hh, gradu_h, window_hh, lse_hh, prefix_hh = operands

        def step(carry, inputs):
            suffix, pend_key, pend_value = carry
            query_blk, key_blk, value_blk, key_tail, value_tail, grad_blk, gradu_blk, window_blk, lse_blk, prefix_blk, coef_row, block_id = inputs
            suffix_b = suffix.astype(jnp.bfloat16)
            lin_weights = jnp.where(causal, matmul(query_blk, key_blk.T) * coef_row[:, None], 0.0).astype(jnp.bfloat16)
            back_lin = jnp.where(causal, matmul(gradu_blk, value_blk.T), 0.0).astype(jnp.bfloat16)
            d_query = matmul(gradu_blk, prefix_blk.T) + matmul(back_lin, key_blk)
            d_key = matmul(back_lin.T, query_blk) + matmul(value_blk, suffix_b.T)
            d_value = matmul(lin_weights.T, grad_blk) + matmul(key_blk, suffix_b)
            key_ext = jnp.concatenate([key_tail, key_blk], 0)
            value_ext = jnp.concatenate([value_tail, value_blk], 0)
            mask = window_mask(block_id)
            logits = matmul(query_blk, key_ext.T) * inv_root
            probs = jnp.where(mask, jnp.exp(logits - lse_blk[:, None]), 0.0)
            d_probs = matmul(grad_blk, value_ext.T)
            delta = lax.optimization_barrier(jnp.sum(grad_blk.astype(jnp.float32) * window_blk, 1))
            d_logits = (probs * (d_probs - delta[:, None]) * inv_root).astype(jnp.bfloat16)
            d_query = d_query + matmul(d_logits, key_ext)
            d_key_ext = matmul(d_logits.T, query_blk)
            d_value_ext = matmul(probs.astype(jnp.bfloat16).T, grad_blk)
            pad_rows = jnp.zeros((TOK_DEV - WINDOW, HEAD_DIM), jnp.float32)
            d_key = d_key + d_key_ext[WINDOW:] + jnp.concatenate([pad_rows, pend_key], 0)
            d_value = d_value + d_value_ext[WINDOW:] + jnp.concatenate([pad_rows, pend_value], 0)
            new_carry = (suffix + matmul(query_blk.T, gradu_blk), d_key_ext[:WINDOW], d_value_ext[:WINDOW])
            return (new_carry, (d_query.astype(jnp.bfloat16), d_key.astype(jnp.bfloat16), d_value.astype(jnp.bfloat16)))
        init = (jnp.zeros((HEAD_DIM, HEAD_DIM), jnp.float32), jnp.zeros((WINDOW, HEAD_DIM), jnp.float32), jnp.zeros((WINDOW, HEAD_DIM), jnp.float32))
        xs = (query_h, key_h, value_h, with_tails(key_h), with_tails(value_h), grad_hh, gradu_h, window_hh, lse_hh, prefix_hh, coef_blocks, block_ids)
        _, results = lax.scan(step, init, xs, reverse=True)
        return results
    dq_h, dk_h, dv_h = lax.map(backward_head, (query_all, key_all, value_all, by_head(grad_h), by_head(grad_u), window_h, lse_h, prefix_h))
    return (output, from_heads(dq_h), from_heads(dk_h), from_heads(dv_h))
```

```python
import functools
import math

import jax
import jax.numpy as jnp
from jax import lax
from jax.experimental import pallas as pl
from jax.experimental.pallas import tpu as pltpu
from jax.sharding import PartitionSpec as P

HEAD_DIM = 128
WINDOW = 256
HALF = 256
EPS = 1e-06
MESH = pl.DeviceIdType.MESH
F32 = jnp.float32
BF16 = jnp.bfloat16


def dot(left, right, left_dim, right_dim):
    return lax.dot_general(
        left, right, (((left_dim,), (right_dim,)), ((), ())), preferred_element_type=F32
    )


def nn(left, right):
    return dot(left, right, 1, 0)


def nt(left, right):
    return dot(left, right, 1, 1)


def tn(left, right):
    return dot(left, right, 0, 0)


def kernel(
    n_ctx, n_z, n_head,
    q_hbm, k_hbm, v_hbm, gain_hbm, cot_hbm,
    out_hbm, dq_hbm, dk_hbm, dv_hbm,
    q, k, v, gain, cot,
    k_halo, v_halo, dk_give, dv_give, dk_take, dv_take,
    scat_f, got_f, back_f, pre, scat_b, got_b, back_b, post, flat,
    stat_mine, stat_all,
    probs, w_own, w_prev, local, scaled_t, grad_t, gradu_t,
    dk_acc, dv_acc, out, dq, dk, dv,
    in_sem, out_sem, scan_send, scan_recv, halo_send, halo_recv, stat_send, stat_recv,
):
    me = lax.axis_index("ctx")
    mine = lax.axis_index("head")
    n_y = n_ctx // n_z
    my_y = me // n_z
    my_z = lax.rem(me, n_z)
    following = lax.rem(me + 1, n_ctx)
    before = lax.rem(me + n_ctx - 1, n_ctx)
    rows = 256 // n_ctx
    tokens = 2 * HALF
    features = 256 * n_head
    scale = 1.0 / math.sqrt(HEAD_DIM)

    barrier = pltpu.get_barrier_semaphore()

    def greet(step, carry):
        pl.semaphore_signal(
            barrier, inc=1, device_id={"ctx": lax.rem(me + step, n_ctx), "head": mine},
            device_id_type=MESH,
        )
        return carry

    lax.fori_loop(1, n_ctx, greet, 0)
    for step in range(1, n_head):
        pl.semaphore_signal(
            barrier, inc=1, device_id={"ctx": me, "head": lax.rem(mine + step, n_head)},
            device_id_type=MESH,
        )

    loads = [
        pltpu.make_async_copy(src, dst, in_sem.at[i])
        for i, (src, dst) in enumerate(
            ((k_hbm, k), (v_hbm, v), (q_hbm, q), (cot_hbm, cot), (gain_hbm, gain))
        )
    ]
    for load in loads:
        load.start()

    y_order = sorted(range(n_y), key=lambda d: -min(d, n_y - d))

    def exchange(src, dst, phase):
        def send(away_y, away_z):
            target = lax.rem(my_y + away_y, n_y) * n_z + lax.rem(my_z + away_z, n_z)
            pltpu.make_async_remote_copy(
                src.at[target], dst.at[me], scan_send.at[phase], scan_recv.at[phase],
                device_id={"ctx": target, "head": mine}, device_id_type=MESH,
            ).start()

        def step(i, carry):
            away_z = n_z // 2 + ((i + 1) // 2) * (1 - 2 * lax.rem(i, 2))
            for away_y in y_order:
                send(away_y, away_z)
            return carry

        lax.fori_loop(0, n_z - 1, step, 0)
        for away_y in y_order:
            if away_y:
                send(away_y, 0)
        dst[pl.ds(me, 1)] = src[pl.ds(me, 1)]

    def arrived(dst, phase):
        part = dst.at[pl.ds(0, n_ctx - 1)]
        pltpu.make_async_copy(part, part, scan_recv.at[phase]).wait()

    def left(src, phase):
        part = src.at[pl.ds(0, n_ctx - 1)]
        pltpu.make_async_copy(part, part, scan_send.at[phase]).wait()

    def scatter(state, head, dst):
        for i in range(HEAD_DIM // rows):
            dst[head * (HEAD_DIM // rows) + i] = state[i * rows : (i + 1) * rows].astype(BF16)

    def running(src, dst, order):
        total = jnp.zeros((rows, HEAD_DIM), F32)
        for i in order:
            dst[i] = total.astype(BF16)
            total = total + src[i].astype(F32)

    def collect(src, dst):
        for i in range(n_ctx):
            dst[i * rows : (i + 1) * rows, :] = src[i].astype(F32)

    cols = [slice(h * HEAD_DIM, (h + 1) * HEAD_DIM) for h in range(2)]
    half = [slice(b * HALF, (b + 1) * HALF) for b in range(2)]

    loads[0].wait()
    loads[1].wait()
    for h in range(2):
        scatter(tn(v[:, cols[h]], k[:, cols[h]]), h, scat_f)
    pl.semaphore_wait(barrier, n_ctx - 1 + n_head - 1)
    exchange(scat_f, got_f, 0)
    halo_out = [
        pltpu.make_async_remote_copy(
            src.at[pl.ds(HALF, HALF)], dst, halo_send.at[i], halo_recv.at[i],
            device_id={"ctx": following, "head": mine}, device_id_type=MESH,
        )
        for i, (src, dst) in enumerate(((k, k_halo), (v, v_halo)))
    ]
    for copy in halo_out:
        copy.start()

    for load in loads[2:]:
        load.wait()
    position = me * tokens + lax.broadcasted_iota(jnp.int32, (1, tokens), 1)
    coef = 1.0 / jnp.sqrt(HEAD_DIM * (position + 1).astype(F32))
    lower = lax.broadcasted_iota(jnp.int32, (HALF, HALF), 0) > lax.broadcasted_iota(
        jnp.int32, (HALF, HALF), 1
    )
    no_halo = jnp.where(me == 0, -1e30, 0.0).astype(F32)
    scaled_t[...] = (gain[...].astype(F32) * cot[...].astype(F32)).T

    def near(b, h, own, halo):
        prev_part = halo[:, cols[h]] if b == 0 else own[half[0], cols[h]]
        return prev_part, own[half[b], cols[h]]

    def forward(b, h):
        query = q[half[b], cols[h]]
        key_prev, key_own = near(b, h, k, k_halo)
        value_prev, value_own = near(b, h, v, v_halo)
        prev = nt(key_prev, query)
        own = nt(key_own, query)
        c = coef[:, half[b]]
        logits = jnp.where(lower, prev + no_halo if b == 0 else prev, own)
        peak = jnp.max(logits, 0, keepdims=True)
        weight = jnp.exp((logits - peak) * scale)
        weight = weight * (1.0 / jnp.sum(weight, 0, keepdims=True))
        probs[h, b] = weight
        mix_own = jnp.where(lower, 0.0, weight + c * own).astype(BF16)
        mix_prev = jnp.where(lower, weight, 0.0)
        if b == 1:
            mix_prev = mix_prev + c * prev
        mix_prev = mix_prev.astype(BF16)
        w_own[h, b] = mix_own
        w_prev[h, b] = mix_prev
        local[cols[h], half[b]] = tn(value_own, mix_own) + tn(value_prev, mix_prev)

    for h in range(2):
        forward(1, h)
    for copy in halo_out:
        copy.wait()
    for h in range(2):
        forward(0, h)

    arrived(got_f, 0)
    running(got_f, back_f, range(n_ctx))
    exchange(back_f, pre, 1)
    arrived(pre, 1)
    collect(pre, flat)
    prefix = flat[...].astype(BF16)

    hidden = []
    for h in range(2):
        hidden.append(local[cols[h], :] + coef * nt(prefix[cols[h], :], q[:, cols[h]]))
    squares = sum(jnp.sum(x * x, 0, keepdims=True) for x in hidden)
    crossed = sum(
        jnp.sum(x * scaled_t[cols[h], :], 0, keepdims=True) for h, x in enumerate(hidden)
    )
    stat_mine[0:1, :] = squares
    stat_mine[1:2, :] = crossed
    shares = [
        pltpu.make_async_remote_copy(
            stat_mine, stat_all.at[mine], stat_send, stat_recv,
            device_id={"ctx": me, "head": lax.rem(mine + step, n_head)}, device_id_type=MESH,
        )
        for step in range(n_head - 1, 0, -1)
    ]
    for copy in shares:
        copy.start()
    stat_all[pl.ds(mine, 1)] = stat_mine[...][None]
    for h in range(2):
        local[cols[h], :] = hidden[h]
    others = stat_all.at[pl.ds(0, n_head - 1)]
    pltpu.make_async_copy(others, others, stat_recv).wait()
    sums = stat_all[0]
    for i in range(1, n_head):
        sums = sums + stat_all[i]
    recip = 1.0 / jnp.sqrt(sums[0:1] / features + EPS)
    pull = recip * recip * recip * sums[1:2] / features

    for h in range(2):
        full = recip * scaled_t[cols[h], :] - local[cols[h], :] * pull
        grad_t[cols[h], :] = full.astype(BF16)
        grad_u = (full * coef).astype(BF16)
        gradu_t[cols[h], :] = grad_u
        scatter(nn(grad_u, q[:, cols[h]]), h, scat_b)
    exchange(scat_b, got_b, 2)

    dk_acc[...] = jnp.zeros_like(dk_acc)
    dv_acc[...] = jnp.zeros_like(dv_acc)

    def backward(b, h):
        query = q[half[b], cols[h]]
        key_prev, key_own = near(b, h, k, k_halo)
        value_prev, value_own = near(b, h, v, v_halo)
        grad = grad_t[cols[h], half[b]]
        c = coef[:, half[b]]
        prev = nn(value_prev, grad)
        own = nn(value_own, grad)
        weight = probs[h, b]
        pulled = jnp.where(lower, prev, own)
        delta = jnp.sum(weight * pulled, 0, keepdims=True)
        d_logits = weight * (pulled - delta) * scale
        d_own = jnp.where(lower, 0.0, d_logits + c * own).astype(BF16)
        d_prev = jnp.where(lower, d_logits, 0.0)
        if b == 1:
            d_prev = d_prev + c * prev
        d_prev = d_prev.astype(BF16)
        far = tn(gradu_t[cols[h], half[b]], prefix[cols[h], :])
        dq[half[b], cols[h]] = (far + tn(d_own, key_own) + tn(d_prev, key_prev)).astype(BF16)
        dk_acc[half[b], cols[h]] += nn(d_own, query)
        dv_acc[half[b], cols[h]] += nt(w_own[h, b], grad)
        if b == 0:
            dk_give[:, cols[h]] = nn(d_prev, query).astype(BF16)
            dv_give[:, cols[h]] = nt(w_prev[h, b], grad).astype(BF16)
        else:
            dk_acc[half[0], cols[h]] += nn(d_prev, query)
            dv_acc[half[0], cols[h]] += nt(w_prev[h, b], grad)

    for h in range(2):
        backward(0, h)
    halo_back = [
        pltpu.make_async_remote_copy(
            src, dst, halo_send.at[2 + i], halo_recv.at[2 + i],
            device_id={"ctx": before, "head": mine}, device_id_type=MESH,
        )
        for i, (src, dst) in enumerate(((dk_give, dk_take), (dv_give, dv_take)))
    ]
    for copy in halo_back:
        copy.start()
    for h in range(2):
        backward(1, h)
    store_dq = pltpu.make_async_copy(dq, dq_hbm, out_sem.at[0])
    store_dq.start()

    arrived(got_b, 2)
    running(got_b, back_b, range(n_ctx - 1, -1, -1))
    exchange(back_b, post, 3)

    out[...] = ((local[...] * recip).T * gain[...].astype(F32)).astype(BF16)
    store_out = pltpu.make_async_copy(out, out_hbm, out_sem.at[1])
    store_out.start()
    for copy in halo_back:
        copy.wait()
    dk_acc[half[1], :] += dk_take[...].astype(F32)
    dv_acc[half[1], :] += dv_take[...].astype(F32)

    arrived(post, 3)
    collect(post, flat)
    suffix = flat[...].astype(BF16)
    for h in range(2):
        dk[:, cols[h]] = (dk_acc[:, cols[h]] + nn(v[:, cols[h]], suffix[cols[h], :])).astype(BF16)
    store_dk = pltpu.make_async_copy(dk, dk_hbm, out_sem.at[2])
    store_dk.start()
    for h in range(2):
        dv[:, cols[h]] = (dv_acc[:, cols[h]] + nt(k[:, cols[h]], suffix[cols[h], :])).astype(BF16)
    store_dv = pltpu.make_async_copy(dv, dv_hbm, out_sem.at[3])
    store_dv.start()

    for phase, src in enumerate((scat_f, back_f, scat_b, back_b)):
        left(src, phase)
    sent = stat_all.at[pl.ds(0, n_head - 1)]
    pltpu.make_async_copy(sent, sent, stat_send).wait()
    for copy in (store_dq, store_out, store_dk, store_dv):
        copy.wait()


def on_device(n_ctx, n_z, n_head, queries, keys, values, gain, cotangent):
    tokens, width = queries.shape
    pieces = (n_ctx, 256 // n_ctx, HEAD_DIM)
    block = jax.ShapeDtypeStruct((tokens, width), BF16)
    wide = pltpu.VMEM((tokens, width), BF16)
    halo = pltpu.VMEM((HALF, width), BF16)
    piece = pltpu.VMEM(pieces, BF16)
    square = (2, 2, HALF, HALF)
    turned = (width, tokens)
    return pl.pallas_call(
        functools.partial(kernel, n_ctx, n_z, n_head),
        out_shape=[block] * 4,
        in_specs=[pl.BlockSpec(memory_space=pl.ANY)] * 5,
        out_specs=[pl.BlockSpec(memory_space=pl.ANY)] * 4,
        scratch_shapes=[
            wide, wide, wide, pltpu.VMEM((1, width), BF16), wide,
            halo, halo, halo, halo, halo, halo,
            piece, piece, piece, piece, piece, piece, piece, piece,
            pltpu.VMEM((256, HEAD_DIM), F32),
            pltpu.VMEM((2, tokens), F32), pltpu.VMEM((n_head, 2, tokens), F32),
            pltpu.VMEM(square, F32), pltpu.VMEM(square, BF16), pltpu.VMEM(square, BF16),
            pltpu.VMEM(turned, F32), pltpu.VMEM(turned, F32),
            pltpu.VMEM(turned, BF16), pltpu.VMEM(turned, BF16),
            pltpu.VMEM((tokens, width), F32), pltpu.VMEM((tokens, width), F32),
            wide, wide, wide, wide,
            pltpu.SemaphoreType.DMA((5,)), pltpu.SemaphoreType.DMA((4,)),
            pltpu.SemaphoreType.DMA((4,)), pltpu.SemaphoreType.DMA((4,)),
            pltpu.SemaphoreType.DMA((4,)), pltpu.SemaphoreType.DMA((4,)),
            pltpu.SemaphoreType.DMA, pltpu.SemaphoreType.DMA,
        ],
        compiler_params=pltpu.CompilerParams(
            collective_id=0, has_side_effects=True, vmem_limit_bytes=48 << 20
        ),
    )(queries, keys, values, gain.reshape(1, width), cotangent)


def solution(mesh):
    n_ctx, n_head = mesh.shape["ctx"], mesh.shape["head"]
    n_z = 16 if n_ctx % 16 == 0 else n_ctx // 2
    return jax.shard_map(
        functools.partial(on_device, n_ctx, n_z, n_head),
        mesh=mesh,
        in_specs=(
            P("ctx", "head"), P("ctx", "head"), P("ctx", "head"), P("head"), P("ctx", "head"),
        ),
        out_specs=(P("ctx", "head"),) * 4,
        check_vma=False,
    )
```

```python
import functools
import math

import jax
import jax.numpy as jnp
from jax import lax
from jax.experimental import pallas as pl
from jax.experimental.pallas import tpu as pltpu
from jax.sharding import PartitionSpec as P

HEAD_DIM = 128
WINDOW = 256
HALF = 256
EPS = 1e-06
MESH = pl.DeviceIdType.MESH
F32 = jnp.float32
BF16 = jnp.bfloat16


def dot(left, right, left_dim, right_dim):
    return lax.dot_general(
        left, right, (((left_dim,), (right_dim,)), ((), ())), preferred_element_type=F32
    )


def nn(left, right):
    return dot(left, right, 1, 0)


def nt(left, right):
    return dot(left, right, 1, 1)


def tn(left, right):
    return dot(left, right, 0, 0)


def kernel(
    n_ctx, n_z, n_head,
    q_hbm, k_hbm, v_hbm, gain_hbm, cot_hbm,
    out, dq, dk_acc, dv_acc, suffix, k, v,
    q, gain, cot,
    k_halo, v_halo, dk_give, dv_give, dk_take, dv_take,
    scat_f, got_f, back_f, pre, scat_b, got_b, back_b, post, flat,
    stat_mine, stat_all,
    probs, w_own, w_prev, local, scaled_t, grad_t, gradu_t,
    in_sem, scan_send, scan_recv, halo_send, halo_recv, stat_send, stat_recv,
):
    me = lax.axis_index("ctx")
    mine = lax.axis_index("head")
    n_y = n_ctx // n_z
    my_y = me // n_z
    my_z = lax.rem(me, n_z)
    following = lax.rem(me + 1, n_ctx)
    before = lax.rem(me + n_ctx - 1, n_ctx)
    rows = 256 // n_ctx
    tokens = 2 * HALF
    features = 256 * n_head
    scale = 1.0 / math.sqrt(HEAD_DIM)

    barrier = pltpu.get_barrier_semaphore()

    y_order = sorted(range(n_y), key=lambda d: -min(d, n_y - d))

    def farthest_first(visit):
        def at(away_y, away_z):
            visit(lax.rem(my_y + away_y, n_y) * n_z + lax.rem(my_z + away_z, n_z))

        def step(i, carry):
            away_z = n_z // 2 + ((i + 1) // 2) * (1 - 2 * lax.rem(i, 2))
            for away_y in y_order:
                at(away_y, away_z)
            return carry

        lax.fori_loop(0, n_z - 1, step, 0)
        for away_y in y_order:
            if away_y:
                at(away_y, 0)

    def greet(target, head):
        pl.semaphore_signal(
            barrier, inc=1, device_id={"ctx": target, "head": head}, device_id_type=MESH
        )

    farthest_first(lambda target: greet(target, mine))
    for step in range(1, n_head):
        greet(me, lax.rem(mine + step, n_head))

    loads = [
        pltpu.make_async_copy(src, dst, in_sem.at[i])
        for i, (src, dst) in enumerate(
            ((k_hbm, k), (v_hbm, v), (q_hbm, q), (cot_hbm, cot), (gain_hbm, gain))
        )
    ]
    for load in loads:
        load.start()

    def exchange(src, dst, phase):
        def send(target):
            pltpu.make_async_remote_copy(
                src.at[target], dst.at[me], scan_send.at[phase], scan_recv.at[phase],
                device_id={"ctx": target, "head": mine}, device_id_type=MESH,
            ).start()

        farthest_first(send)
        dst[pl.ds(me, 1)] = src[pl.ds(me, 1)]

    def arrived(dst, phase):
        part = dst.at[pl.ds(0, n_ctx - 1)]
        pltpu.make_async_copy(part, part, scan_recv.at[phase]).wait()

    def left(src, phase):
        part = src.at[pl.ds(0, n_ctx - 1)]
        pltpu.make_async_copy(part, part, scan_send.at[phase]).wait()

    def scatter(state, head, dst):
        for i in range(HEAD_DIM // rows):
            dst[head * (HEAD_DIM // rows) + i] = state[i * rows : (i + 1) * rows].astype(BF16)

    def running(src, dst, order):
        total = jnp.zeros((rows, HEAD_DIM), F32)
        for i in order:
            dst[i] = total.astype(BF16)
            total = total + src[i].astype(F32)

    def collect(src, dst):
        for i in range(n_ctx):
            dst[i * rows : (i + 1) * rows, :] = src[i].astype(F32)

    cols = [slice(h * HEAD_DIM, (h + 1) * HEAD_DIM) for h in range(2)]
    half = [slice(b * HALF, (b + 1) * HALF) for b in range(2)]

    loads[0].wait()
    loads[1].wait()
    for h in range(2):
        scatter(tn(v[:, cols[h]], k[:, cols[h]]), h, scat_f)
    pl.semaphore_wait(barrier, n_ctx - 1 + n_head - 1)
    exchange(scat_f, got_f, 0)
    halo_out = [
        pltpu.make_async_remote_copy(
            src.at[pl.ds(HALF, HALF)], dst, halo_send.at[i], halo_recv.at[i],
            device_id={"ctx": following, "head": mine}, device_id_type=MESH,
        )
        for i, (src, dst) in enumerate(((k, k_halo), (v, v_halo)))
    ]
    for copy in halo_out:
        copy.start()

    for load in loads[2:]:
        load.wait()
    position = me * tokens + lax.broadcasted_iota(jnp.int32, (1, tokens), 1)
    coef = 1.0 / jnp.sqrt(HEAD_DIM * (position + 1).astype(F32))
    lower = lax.broadcasted_iota(jnp.int32, (HALF, HALF), 0) > lax.broadcasted_iota(
        jnp.int32, (HALF, HALF), 1
    )
    no_halo = jnp.where(me == 0, -1e30, 0.0).astype(F32)
    scaled_t[...] = (gain[...].astype(F32).reshape(1, 256) * cot[...].astype(F32)).T

    def near(b, h, own, halo):
        prev_part = halo[:, cols[h]] if b == 0 else own[half[0], cols[h]]
        return prev_part, own[half[b], cols[h]]

    def forward(b, h):
        query = q[half[b], cols[h]]
        key_prev, key_own = near(b, h, k, k_halo)
        value_prev, value_own = near(b, h, v, v_halo)
        prev = nt(key_prev, query)
        own = nt(key_own, query)
        c = coef[:, half[b]]
        logits = jnp.where(lower, prev + no_halo if b == 0 else prev, own)
        peak = jnp.max(logits, 0, keepdims=True)
        weight = jnp.exp((logits - peak) * scale)
        weight = weight * (1.0 / jnp.sum(weight, 0, keepdims=True))
        probs[h, b] = weight
        mix_own = jnp.where(lower, 0.0, weight + c * own).astype(BF16)
        mix_prev = jnp.where(lower, weight, 0.0)
        if b == 1:
            mix_prev = mix_prev + c * prev
        mix_prev = mix_prev.astype(BF16)
        w_own[h, b] = mix_own
        w_prev[h, b] = mix_prev
        local[cols[h], half[b]] = tn(value_own, mix_own) + tn(value_prev, mix_prev)

    for h in range(2):
        forward(1, h)
    for copy in halo_out:
        copy.wait()
    for h in range(2):
        forward(0, h)

    arrived(got_f, 0)
    running(got_f, back_f, range(n_ctx))
    exchange(back_f, pre, 1)
    arrived(pre, 1)
    collect(pre, flat)
    prefix = flat[...].astype(BF16)

    hidden = []
    for h in range(2):
        hidden.append(local[cols[h], :] + coef * nt(prefix[cols[h], :], q[:, cols[h]]))
    squares = sum(jnp.sum(x * x, 0, keepdims=True) for x in hidden)
    crossed = sum(
        jnp.sum(x * scaled_t[cols[h], :], 0, keepdims=True) for h, x in enumerate(hidden)
    )
    stat_mine[0:1, :] = squares
    stat_mine[1:2, :] = crossed
    shares = [
        pltpu.make_async_remote_copy(
            stat_mine, stat_all.at[mine], stat_send, stat_recv,
            device_id={"ctx": me, "head": lax.rem(mine + step, n_head)}, device_id_type=MESH,
        )
        for step in range(n_head - 1, 0, -1)
    ]
    for copy in shares:
        copy.start()
    stat_all[pl.ds(mine, 1)] = stat_mine[...][None]
    for h in range(2):
        local[cols[h], :] = hidden[h]
    others = stat_all.at[pl.ds(0, n_head - 1)]
    pltpu.make_async_copy(others, others, stat_recv).wait()
    sums = stat_all[0]
    for i in range(1, n_head):
        sums = sums + stat_all[i]
    recip = 1.0 / jnp.sqrt(sums[0:1] / features + EPS)
    pull = recip * recip * recip * sums[1:2] / features

    for h in range(2):
        full = recip * scaled_t[cols[h], :] - local[cols[h], :] * pull
        grad_t[cols[h], :] = full.astype(BF16)
        grad_u = (full * coef).astype(BF16)
        gradu_t[cols[h], :] = grad_u
        scatter(nn(grad_u, q[:, cols[h]]), h, scat_b)
    exchange(scat_b, got_b, 2)

    dk_acc[...] = jnp.zeros_like(dk_acc)
    dv_acc[...] = jnp.zeros_like(dv_acc)

    def backward(b, h):
        query = q[half[b], cols[h]]
        key_prev, key_own = near(b, h, k, k_halo)
        value_prev, value_own = near(b, h, v, v_halo)
        grad = grad_t[cols[h], half[b]]
        c = coef[:, half[b]]
        prev = nn(value_prev, grad)
        own = nn(value_own, grad)
        weight = probs[h, b]
        pulled = jnp.where(lower, prev, own)
        delta = jnp.sum(weight * pulled, 0, keepdims=True)
        d_logits = weight * (pulled - delta) * scale
        d_own = jnp.where(lower, 0.0, d_logits + c * own).astype(BF16)
        d_prev = jnp.where(lower, d_logits, 0.0)
        if b == 1:
            d_prev = d_prev + c * prev
        d_prev = d_prev.astype(BF16)
        far = tn(gradu_t[cols[h], half[b]], prefix[cols[h], :])
        dq[half[b], cols[h]] = (far + tn(d_own, key_own) + tn(d_prev, key_prev)).astype(BF16)
        dk_acc[half[b], cols[h]] += nn(d_own, query)
        dv_acc[half[b], cols[h]] += nt(w_own[h, b], grad)
        if b == 0:
            dk_give[:, cols[h]] = nn(d_prev, query).astype(BF16)
            dv_give[:, cols[h]] = nt(w_prev[h, b], grad).astype(BF16)
        else:
            dk_acc[half[0], cols[h]] += nn(d_prev, query)
            dv_acc[half[0], cols[h]] += nt(w_prev[h, b], grad)

    for h in range(2):
        backward(0, h)
    halo_back = [
        pltpu.make_async_remote_copy(
            src, dst, halo_send.at[2 + i], halo_recv.at[2 + i],
            device_id={"ctx": before, "head": mine}, device_id_type=MESH,
        )
        for i, (src, dst) in enumerate(((dk_give, dk_take), (dv_give, dv_take)))
    ]
    for copy in halo_back:
        copy.start()
    for h in range(2):
        backward(1, h)

    arrived(got_b, 2)
    running(got_b, back_b, range(n_ctx - 1, -1, -1))
    exchange(back_b, post, 3)

    out[...] = ((local[...] * recip).T * gain[...].astype(F32).reshape(1, 256)).astype(BF16)
    for copy in halo_back:
        copy.wait()
    dk_acc[half[1], :] += dk_take[...].astype(F32)
    dv_acc[half[1], :] += dv_take[...].astype(F32)

    arrived(post, 3)
    collect(post, flat)
    suffix[...] = flat[...].astype(BF16)
    for phase, src in enumerate((scat_f, back_f, scat_b, back_b)):
        left(src, phase)
    sent = stat_all.at[pl.ds(0, n_head - 1)]
    pltpu.make_async_copy(sent, sent, stat_send).wait()


def finish(out, dq, dk_acc, dv_acc, suffix, k, v, out_hbm, dq_hbm, dk_hbm, dv_hbm, dk, dv, sem):
    stores = [
        pltpu.make_async_copy(src, dst, sem.at[i])
        for i, (src, dst) in enumerate(((out, out_hbm), (dq, dq_hbm), (dk, dk_hbm), (dv, dv_hbm)))
    ]
    stores[0].start()
    stores[1].start()
    cols = [slice(h * HEAD_DIM, (h + 1) * HEAD_DIM) for h in range(2)]
    for c in cols:
        dk[:, c] = (dk_acc[:, c] + nn(v[:, c], suffix[c, :])).astype(BF16)
    stores[2].start()
    for c in cols:
        dv[:, c] = (dv_acc[:, c] + nt(k[:, c], suffix[c, :])).astype(BF16)
    stores[3].start()
    for store in stores:
        store.wait()


def on_device(n_ctx, n_z, n_head, queries, keys, values, gain, cotangent):
    tokens, width = queries.shape
    pieces = (n_ctx, 256 // n_ctx, HEAD_DIM)
    block = jax.ShapeDtypeStruct((tokens, width), BF16)
    wide = pltpu.VMEM((tokens, width), BF16)
    halo = pltpu.VMEM((HALF, width), BF16)
    piece = pltpu.VMEM(pieces, BF16)
    square = (2, 2, HALF, HALF)
    turned = (width, tokens)
    operands = (queries, keys, values, gain, cotangent)
    summed = jax.ShapeDtypeStruct((tokens, width), F32)
    vmem = pl.BlockSpec(memory_space=pltpu.VMEM)
    anywhere = pl.BlockSpec(memory_space=pl.ANY)
    results = pl.pallas_call(
        functools.partial(kernel, n_ctx, n_z, n_head),
        out_shape=[
            block, block, summed, summed, jax.ShapeDtypeStruct((width, HEAD_DIM), BF16), block,
            block,
        ],
        in_specs=[anywhere] * 5,
        out_specs=[vmem] * 7,
        scratch_shapes=[
            wide, pltpu.VMEM((width,), BF16), wide,
            halo, halo, halo, halo, halo, halo,
            piece, piece, piece, piece, piece, piece, piece, piece,
            pltpu.VMEM((256, HEAD_DIM), F32),
            pltpu.VMEM((2, tokens), F32), pltpu.VMEM((n_head, 2, tokens), F32),
            pltpu.VMEM(square, F32), pltpu.VMEM(square, BF16), pltpu.VMEM(square, BF16),
            pltpu.VMEM(turned, F32), pltpu.VMEM(turned, F32),
            pltpu.VMEM(turned, BF16), pltpu.VMEM(turned, BF16),
            pltpu.SemaphoreType.DMA((5,)),
            pltpu.SemaphoreType.DMA((4,)), pltpu.SemaphoreType.DMA((4,)),
            pltpu.SemaphoreType.DMA((4,)), pltpu.SemaphoreType.DMA((4,)),
            pltpu.SemaphoreType.DMA, pltpu.SemaphoreType.DMA,
        ],
        compiler_params=pltpu.CompilerParams(
            collective_id=0, has_side_effects=True, vmem_limit_bytes=48 << 20
        ),
    )(*[pltpu.with_memory_space_constraint(x, pltpu.HBM) for x in operands])
    return pl.pallas_call(
        finish,
        out_shape=[block] * 4,
        in_specs=[vmem] * 7,
        out_specs=[anywhere] * 4,
        scratch_shapes=[wide, wide, pltpu.SemaphoreType.DMA((4,))],
        compiler_params=pltpu.CompilerParams(vmem_limit_bytes=32 << 20),
    )(*[pltpu.with_memory_space_constraint(x, pltpu.VMEM) for x in results])


def solution(mesh):
    n_ctx, n_head = mesh.shape["ctx"], mesh.shape["head"]
    n_z = 16 if n_ctx % 16 == 0 else n_ctx // 2
    return jax.shard_map(
        functools.partial(on_device, n_ctx, n_z, n_head),
        mesh=mesh,
        in_specs=(
            P("ctx", "head"), P("ctx", "head"), P("ctx", "head"), P("head"), P("ctx", "head"),
        ),
        out_specs=(P("ctx", "head"),) * 4,
        check_vma=False,
    )
```

```python
import functools
import math

import jax
import jax.numpy as jnp
from jax import lax
from jax.experimental import pallas as pl
from jax.experimental.pallas import tpu as pltpu
from jax.sharding import PartitionSpec as P

HEAD_DIM = 128
WINDOW = 256
HALF = 256
EPS = 1e-06
MESH = pl.DeviceIdType.MESH
F32 = jnp.float32
BF16 = jnp.bfloat16


def dot(left, right, left_dim, right_dim):
    return lax.dot_general(
        left, right, (((left_dim,), (right_dim,)), ((), ())), preferred_element_type=F32
    )


def nn(left, right):
    return dot(left, right, 1, 0)


def nt(left, right):
    return dot(left, right, 1, 1)


def tn(left, right):
    return dot(left, right, 0, 0)


def kernel(
    n_ctx, n_z, n_head,
    q_hbm, k_hbm, v_hbm, gain_hbm, cot_hbm,
    out, dq, dk_acc, dv_acc, suffix, k, v,
    q, gain, cot,
    k_halo, v_halo, dk_give, dv_give, dk_take, dv_take,
    scat_f, mid, got_f, back_f, pre, scat_b, got_b, back_b, post, flat,
    stat_mine, stat_all,
    probs, w_own, w_prev, local, scaled_t, grad_t, gradu_t,
    in_sem, leg_send, leg_recv, known, scan_send, scan_recv, halo_send, halo_recv, stat_send, stat_recv,
):
    me = lax.axis_index("ctx")
    mine = lax.axis_index("head")
    n_y = n_ctx // n_z
    my_y = me // n_z
    my_z = lax.rem(me, n_z)
    following = lax.rem(me + 1, n_ctx)
    before = lax.rem(me + n_ctx - 1, n_ctx)
    rows = 256 // n_ctx
    tokens = 2 * HALF
    features = 256 * n_head
    scale = 1.0 / math.sqrt(HEAD_DIM)

    barrier = pltpu.get_barrier_semaphore()

    reach = max(1, n_z // 4)

    def at_z(step):
        return my_y * n_z + lax.rem(my_z + step, n_z)

    y_order = sorted(range(n_y), key=lambda d: -min(d, n_y - d))

    def farthest_first(visit):
        def at(away_y, away_z):
            visit(lax.rem(my_y + away_y, n_y) * n_z + lax.rem(my_z + away_z, n_z))

        def step(i, carry):
            away_z = n_z // 2 + ((i + 1) // 2) * (1 - 2 * lax.rem(i, 2))
            for away_y in y_order:
                at(away_y, away_z)
            return carry

        lax.fori_loop(0, n_z - 1, step, 0)
        for away_y in y_order:
            if away_y:
                at(away_y, 0)

    def greet(target, head):
        pl.semaphore_signal(
            barrier, inc=1, device_id={"ctx": target, "head": head}, device_id_type=MESH
        )

    for step in range(1, n_y):
        greet(lax.rem(my_y + step, n_y) * n_z + my_z, mine)
    for step in range(reach, 0, -1):
        greet(at_z(step), mine)
        greet(at_z(n_z - step), mine)
    for step in range(1, n_head):
        greet(me, lax.rem(mine + step, n_head))
    greet(following, mine)
    greet(before, mine)

    loads = [
        pltpu.make_async_copy(src, dst, in_sem.at[i])
        for i, (src, dst) in enumerate(
            ((k_hbm, k), (v_hbm, v), (q_hbm, q), (cot_hbm, cot), (gain_hbm, gain))
        )
    ]
    for load in loads:
        load.start()

    def exchange(src, dst, phase):
        def send(target):
            pltpu.make_async_remote_copy(
                src.at[target], dst.at[me], scan_send.at[phase], scan_recv.at[phase],
                device_id={"ctx": target, "head": mine}, device_id_type=MESH,
            ).start()

        farthest_first(send)
        dst[pl.ds(me, 1)] = src[pl.ds(me, 1)]

    def arrived(dst, phase):
        part = dst.at[pl.ds(0, n_ctx - 1)]
        pltpu.make_async_copy(part, part, scan_recv.at[phase]).wait()

    def left(src, phase):
        part = src.at[pl.ds(0, n_ctx - 1)]
        pltpu.make_async_copy(part, part, scan_send.at[phase]).wait()

    def scatter(state, head, dst):
        for i in range(HEAD_DIM // rows):
            dst[head * (HEAD_DIM // rows) + i] = state[i * rows : (i + 1) * rows].astype(BF16)

    def running(src, dst, order):
        total = jnp.zeros((rows, HEAD_DIM), F32)
        for i in order:
            dst[i] = total.astype(BF16)
            total = total + src(i).astype(F32)

    def collect(src, dst):
        for i in range(n_ctx):
            dst[i * rows : (i + 1) * rows, :] = src[i].astype(F32)

    cols = [slice(h * HEAD_DIM, (h + 1) * HEAD_DIM) for h in range(2)]
    half = [slice(b * HALF, (b + 1) * HALF) for b in range(2)]

    loads[0].wait()
    loads[1].wait()
    for h in range(2):
        scatter(tn(v[:, cols[h]], k[:, cols[h]]), h, scat_f)
    pl.semaphore_wait(barrier, n_y - 1 + 2 * reach + n_head - 1 + 2)
    for step in range(1, n_y):
        other = lax.rem(my_y + step, n_y)
        pltpu.make_async_remote_copy(
            scat_f.at[pl.ds(other * n_z, n_z)], mid.at[my_y], leg_send.at[0], leg_recv.at[0],
            device_id={"ctx": other * n_z + my_z, "head": mine}, device_id_type=MESH,
        ).start()
    for step in (reach, n_z - reach):
        pl.semaphore_signal(
            known, inc=1, device_id={"ctx": at_z(step), "head": mine}, device_id_type=MESH
        )
    mid[pl.ds(my_y, 1)] = scat_f[pl.ds(my_y * n_z, n_z)][None]
    for load in loads[2:]:
        load.wait()
    position = me * tokens + lax.broadcasted_iota(jnp.int32, (1, tokens), 1)
    coef = 1.0 / jnp.sqrt(HEAD_DIM * (position + 1).astype(F32))
    lower = lax.broadcasted_iota(jnp.int32, (HALF, HALF), 0) > lax.broadcasted_iota(
        jnp.int32, (HALF, HALF), 1
    )
    no_halo = jnp.where(me == 0, -1e30, 0.0).astype(F32)
    scaled_t[...] = (gain[...].astype(F32).reshape(1, 256) * cot[...].astype(F32)).T

    def near(b, h, own, halo):
        prev_part = halo[:, cols[h]] if b == 0 else own[half[0], cols[h]]
        return prev_part, own[half[b], cols[h]]

    def forward(b, h):
        query = q[half[b], cols[h]]
        key_prev, key_own = near(b, h, k, k_halo)
        value_prev, value_own = near(b, h, v, v_halo)
        prev = nt(key_prev, query)
        own = nt(key_own, query)
        c = coef[:, half[b]]
        logits = jnp.where(lower, prev + no_halo if b == 0 else prev, own)
        peak = jnp.max(logits, 0, keepdims=True)
        weight = jnp.exp((logits - peak) * scale)
        weight = weight * (1.0 / jnp.sum(weight, 0, keepdims=True))
        probs[h, b] = weight
        mix_own = jnp.where(lower, 0.0, weight + c * own).astype(BF16)
        mix_prev = jnp.where(lower, weight, 0.0)
        if b == 1:
            mix_prev = mix_prev + c * prev
        mix_prev = mix_prev.astype(BF16)
        w_own[h, b] = mix_own
        w_prev[h, b] = mix_prev
        local[cols[h], half[b]] = tn(value_own, mix_own) + tn(value_prev, mix_prev)

    for h in range(2):
        forward(1, h)
    whole = mid.at[pl.ds(0, n_y - 1)]
    pltpu.make_async_copy(whole, whole, leg_recv.at[0]).wait()
    pl.semaphore_wait(known, 2)
    for step in sorted(range(1, n_z), key=lambda d: -min(d, n_z - d)):
        other = lax.rem(my_z + step, n_z)
        pltpu.make_async_remote_copy(
            mid.at[:, other], got_f.at[my_z], leg_send.at[1], leg_recv.at[1],
            device_id={"ctx": at_z(step), "head": mine}, device_id_type=MESH,
        ).start()
    got_f[pl.ds(my_z, 1)] = mid[:, pl.ds(my_z, 1)].reshape(1, n_y, rows, HEAD_DIM)
    halo_out = [
        pltpu.make_async_remote_copy(
            src.at[pl.ds(HALF, HALF)], dst, halo_send.at[i], halo_recv.at[i],
            device_id={"ctx": following, "head": mine}, device_id_type=MESH,
        )
        for i, (src, dst) in enumerate(((k, k_halo), (v, v_halo)))
    ]
    for copy in halo_out:
        copy.start()

    for copy in halo_out:
        copy.wait()
    for h in range(2):
        forward(0, h)

    part = got_f.at[pl.ds(0, n_z - 1)]
    pltpu.make_async_copy(part, part, leg_recv.at[1]).wait()
    running(lambda i: got_f[i % n_z, i // n_z], back_f, range(n_ctx))
    exchange(back_f, pre, 0)
    arrived(pre, 0)
    collect(pre, flat)
    prefix = flat[...].astype(BF16)

    hidden = []
    for h in range(2):
        hidden.append(local[cols[h], :] + coef * nt(prefix[cols[h], :], q[:, cols[h]]))
    squares = sum(jnp.sum(x * x, 0, keepdims=True) for x in hidden)
    crossed = sum(
        jnp.sum(x * scaled_t[cols[h], :], 0, keepdims=True) for h, x in enumerate(hidden)
    )
    stat_mine[0:1, :] = squares
    stat_mine[1:2, :] = crossed
    shares = [
        pltpu.make_async_remote_copy(
            stat_mine, stat_all.at[mine], stat_send, stat_recv,
            device_id={"ctx": me, "head": lax.rem(mine + step, n_head)}, device_id_type=MESH,
        )
        for step in range(n_head - 1, 0, -1)
    ]
    for copy in shares:
        copy.start()
    stat_all[pl.ds(mine, 1)] = stat_mine[...][None]
    for h in range(2):
        local[cols[h], :] = hidden[h]
    others = stat_all.at[pl.ds(0, n_head - 1)]
    pltpu.make_async_copy(others, others, stat_recv).wait()
    sums = stat_all[0]
    for i in range(1, n_head):
        sums = sums + stat_all[i]
    recip = 1.0 / jnp.sqrt(sums[0:1] / features + EPS)
    pull = recip * recip * recip * sums[1:2] / features

    for h in range(2):
        full = recip * scaled_t[cols[h], :] - local[cols[h], :] * pull
        grad_t[cols[h], :] = full.astype(BF16)
        grad_u = (full * coef).astype(BF16)
        gradu_t[cols[h], :] = grad_u
        scatter(nn(grad_u, q[:, cols[h]]), h, scat_b)
    exchange(scat_b, got_b, 1)

    dk_acc[...] = jnp.zeros_like(dk_acc)
    dv_acc[...] = jnp.zeros_like(dv_acc)

    def backward(b, h):
        query = q[half[b], cols[h]]
        key_prev, key_own = near(b, h, k, k_halo)
        value_prev, value_own = near(b, h, v, v_halo)
        grad = grad_t[cols[h], half[b]]
        c = coef[:, half[b]]
        prev = nn(value_prev, grad)
        own = nn(value_own, grad)
        weight = probs[h, b]
        pulled = jnp.where(lower, prev, own)
        delta = jnp.sum(weight * pulled, 0, keepdims=True)
        d_logits = weight * (pulled - delta) * scale
        d_own = jnp.where(lower, 0.0, d_logits + c * own).astype(BF16)
        d_prev = jnp.where(lower, d_logits, 0.0)
        if b == 1:
            d_prev = d_prev + c * prev
        d_prev = d_prev.astype(BF16)
        far = tn(gradu_t[cols[h], half[b]], prefix[cols[h], :])
        dq[half[b], cols[h]] = (far + tn(d_own, key_own) + tn(d_prev, key_prev)).astype(BF16)
        dk_acc[half[b], cols[h]] += nn(d_own, query)
        dv_acc[half[b], cols[h]] += nt(w_own[h, b], grad)
        if b == 0:
            dk_give[:, cols[h]] = nn(d_prev, query).astype(BF16)
            dv_give[:, cols[h]] = nt(w_prev[h, b], grad).astype(BF16)
        else:
            dk_acc[half[0], cols[h]] += nn(d_prev, query)
            dv_acc[half[0], cols[h]] += nt(w_prev[h, b], grad)

    for h in range(2):
        backward(0, h)
    halo_back = [
        pltpu.make_async_remote_copy(
            src, dst, halo_send.at[2 + i], halo_recv.at[2 + i],
            device_id={"ctx": before, "head": mine}, device_id_type=MESH,
        )
        for i, (src, dst) in enumerate(((dk_give, dk_take), (dv_give, dv_take)))
    ]
    for copy in halo_back:
        copy.start()
    for h in range(2):
        backward(1, h)

    arrived(got_b, 1)
    running(lambda i: got_b[i], back_b, range(n_ctx - 1, -1, -1))
    exchange(back_b, post, 2)

    out[...] = ((local[...] * recip).T * gain[...].astype(F32).reshape(1, 256)).astype(BF16)
    for copy in halo_back:
        copy.wait()
    dk_acc[half[1], :] += dk_take[...].astype(F32)
    dv_acc[half[1], :] += dv_take[...].astype(F32)

    arrived(post, 2)
    collect(post, flat)
    suffix[...] = flat[...].astype(BF16)
    for phase, src in enumerate((back_f, scat_b, back_b)):
        left(src, phase)
    pltpu.make_async_copy(whole, whole, leg_send.at[0]).wait()
    pltpu.make_async_copy(part, part, leg_send.at[1]).wait()
    sent = stat_all.at[pl.ds(0, n_head - 1)]
    pltpu.make_async_copy(sent, sent, stat_send).wait()


def finish(out, dq, dk_acc, dv_acc, suffix, k, v, out_hbm, dq_hbm, dk_hbm, dv_hbm, dk, dv, sem):
    stores = [
        pltpu.make_async_copy(src, dst, sem.at[i])
        for i, (src, dst) in enumerate(((out, out_hbm), (dq, dq_hbm), (dk, dk_hbm), (dv, dv_hbm)))
    ]
    stores[0].start()
    stores[1].start()
    cols = [slice(h * HEAD_DIM, (h + 1) * HEAD_DIM) for h in range(2)]
    for c in cols:
        dk[:, c] = (dk_acc[:, c] + nn(v[:, c], suffix[c, :])).astype(BF16)
    stores[2].start()
    for c in cols:
        dv[:, c] = (dv_acc[:, c] + nt(k[:, c], suffix[c, :])).astype(BF16)
    stores[3].start()
    for store in stores:
        store.wait()


def on_device(n_ctx, n_z, n_head, queries, keys, values, gain, cotangent):
    tokens, width = queries.shape
    n_y = n_ctx // n_z
    pieces = (n_ctx, 256 // n_ctx, HEAD_DIM)
    block = jax.ShapeDtypeStruct((tokens, width), BF16)
    wide = pltpu.VMEM((tokens, width), BF16)
    halo = pltpu.VMEM((HALF, width), BF16)
    piece = pltpu.VMEM(pieces, BF16)
    square = (2, 2, HALF, HALF)
    turned = (width, tokens)
    operands = (queries, keys, values, gain, cotangent)
    summed = jax.ShapeDtypeStruct((tokens, width), F32)
    vmem = pl.BlockSpec(memory_space=pltpu.VMEM)
    anywhere = pl.BlockSpec(memory_space=pl.ANY)
    results = pl.pallas_call(
        functools.partial(kernel, n_ctx, n_z, n_head),
        out_shape=[
            block, block, summed, summed, jax.ShapeDtypeStruct((width, HEAD_DIM), BF16), block,
            block,
        ],
        in_specs=[anywhere] * 5,
        out_specs=[vmem] * 7,
        scratch_shapes=[
            wide, pltpu.VMEM((width,), BF16), wide,
            halo, halo, halo, halo, halo, halo,
            piece, pltpu.VMEM((n_y, n_z, *pieces[1:]), BF16),
            pltpu.VMEM((n_z, n_y, *pieces[1:]), BF16), piece, piece, piece, piece, piece, piece,
            pltpu.VMEM((256, HEAD_DIM), F32),
            pltpu.VMEM((2, tokens), F32), pltpu.VMEM((n_head, 2, tokens), F32),
            pltpu.VMEM(square, F32), pltpu.VMEM(square, BF16), pltpu.VMEM(square, BF16),
            pltpu.VMEM(turned, F32), pltpu.VMEM(turned, F32),
            pltpu.VMEM(turned, BF16), pltpu.VMEM(turned, BF16),
            pltpu.SemaphoreType.DMA((5,)),
            pltpu.SemaphoreType.DMA((2,)), pltpu.SemaphoreType.DMA((2,)),
            pltpu.SemaphoreType.REGULAR,
            pltpu.SemaphoreType.DMA((3,)), pltpu.SemaphoreType.DMA((3,)),
            pltpu.SemaphoreType.DMA((4,)), pltpu.SemaphoreType.DMA((4,)),
            pltpu.SemaphoreType.DMA, pltpu.SemaphoreType.DMA,
        ],
        compiler_params=pltpu.CompilerParams(
            collective_id=0, has_side_effects=True, vmem_limit_bytes=48 << 20
        ),
    )(*[pltpu.with_memory_space_constraint(x, pltpu.HBM) for x in operands])
    return pl.pallas_call(
        finish,
        out_shape=[block] * 4,
        in_specs=[vmem] * 7,
        out_specs=[anywhere] * 4,
        scratch_shapes=[wide, wide, pltpu.SemaphoreType.DMA((4,))],
        compiler_params=pltpu.CompilerParams(vmem_limit_bytes=32 << 20),
    )(*[pltpu.with_memory_space_constraint(x, pltpu.VMEM) for x in results])


def solution(mesh):
    n_ctx, n_head = mesh.shape["ctx"], mesh.shape["head"]
    n_z = 16 if n_ctx % 16 == 0 else n_ctx // 2
    return jax.shard_map(
        functools.partial(on_device, n_ctx, n_z, n_head),
        mesh=mesh,
        in_specs=(
            P("ctx", "head"), P("ctx", "head"), P("ctx", "head"), P("head"), P("ctx", "head"),
        ),
        out_specs=(P("ctx", "head"),) * 4,
        check_vma=False,
    )
```

```python
import functools
import math

import jax
import jax.numpy as jnp
from jax import lax
from jax.experimental import pallas as pl
from jax.experimental.pallas import tpu as pltpu
from jax.sharding import PartitionSpec as P

HEAD_DIM = 128
WINDOW = 256
HALF = 256
EPS = 1e-06
MESH = pl.DeviceIdType.MESH
F32 = jnp.float32
BF16 = jnp.bfloat16


def dot(left, right, left_dim, right_dim):
    return lax.dot_general(
        left, right, (((left_dim,), (right_dim,)), ((), ())), preferred_element_type=F32
    )


def nn(left, right):
    return dot(left, right, 1, 0)


def nt(left, right):
    return dot(left, right, 1, 1)


def tn(left, right):
    return dot(left, right, 0, 0)


def kernel(
    n_ctx, n_z, n_head,
    q_hbm, k_hbm, v_hbm, gain_hbm, cot_hbm,
    out, dq, dk_acc, dv_acc, suffix, k, v,
    q, gain, cot,
    k_halo, v_halo, dk_give, dv_give, dk_take, dv_take,
    scat_f, mid, got_f, back_f, pre, scat_b, got_b, back_b, post, flat,
    stat_mine, stat_all,
    probs, w_own, w_prev, local, scaled_t, grad_t, gradu_t,
    in_sem, leg_send, leg_recv, known, scan_send, scan_recv, halo_send, halo_recv, stat_send, stat_recv,
):
    me = lax.axis_index("ctx")
    mine = lax.axis_index("head")
    n_y = n_ctx // n_z
    my_y = me // n_z
    my_z = lax.rem(me, n_z)
    following = lax.rem(me + 1, n_ctx)
    before = lax.rem(me + n_ctx - 1, n_ctx)
    rows = 256 // n_ctx
    tokens = 2 * HALF
    features = 256 * n_head
    scale = 1.0 / math.sqrt(HEAD_DIM)

    barrier = pltpu.get_barrier_semaphore()

    reach = max(1, n_z // 8)
    relays = []
    while reach << len(relays) < n_z // 2:
        relays.append(reach << len(relays))

    def at_z(step):
        return my_y * n_z + lax.rem(my_z + step, n_z)

    y_order = sorted(range(n_y), key=lambda d: -min(d, n_y - d))

    def farthest_first(visit):
        def at(away_y, away_z):
            visit(lax.rem(my_y + away_y, n_y) * n_z + lax.rem(my_z + away_z, n_z))

        def step(i, carry):
            away_z = n_z // 2 + ((i + 1) // 2) * (1 - 2 * lax.rem(i, 2))
            for away_y in y_order:
                at(away_y, away_z)
            return carry

        lax.fori_loop(0, n_z - 1, step, 0)
        for away_y in y_order:
            if away_y:
                at(away_y, 0)

    def greet(target, head):
        pl.semaphore_signal(
            barrier, inc=1, device_id={"ctx": target, "head": head}, device_id_type=MESH
        )

    for step in range(1, n_y):
        greet(lax.rem(my_y + step, n_y) * n_z + my_z, mine)
    for step in range(reach, 0, -1):
        greet(at_z(step), mine)
        greet(at_z(n_z - step), mine)
    for step in range(1, n_head):
        greet(me, lax.rem(mine + step, n_head))
    greet(following, mine)
    greet(before, mine)

    loads = [
        pltpu.make_async_copy(src, dst, in_sem.at[i])
        for i, (src, dst) in enumerate(
            ((k_hbm, k), (v_hbm, v), (q_hbm, q), (cot_hbm, cot), (gain_hbm, gain))
        )
    ]
    for load in loads:
        load.start()

    def exchange(src, dst, phase):
        def send(target):
            pltpu.make_async_remote_copy(
                src.at[target], dst.at[me], scan_send.at[phase], scan_recv.at[phase],
                device_id={"ctx": target, "head": mine}, device_id_type=MESH,
            ).start()

        farthest_first(send)
        dst[pl.ds(me, 1)] = src[pl.ds(me, 1)]

    def arrived(dst, phase):
        part = dst.at[pl.ds(0, n_ctx - 1)]
        pltpu.make_async_copy(part, part, scan_recv.at[phase]).wait()

    def left(src, phase):
        part = src.at[pl.ds(0, n_ctx - 1)]
        pltpu.make_async_copy(part, part, scan_send.at[phase]).wait()

    def scatter(state, head, dst):
        for i in range(HEAD_DIM // rows):
            dst[head * (HEAD_DIM // rows) + i] = state[i * rows : (i + 1) * rows].astype(BF16)

    def running(src, dst, order):
        total = jnp.zeros((rows, HEAD_DIM), F32)
        for i in order:
            dst[i] = total.astype(BF16)
            total = total + src(i).astype(F32)

    def collect(src, dst):
        for i in range(n_ctx):
            dst[i * rows : (i + 1) * rows, :] = src[i].astype(F32)

    cols = [slice(h * HEAD_DIM, (h + 1) * HEAD_DIM) for h in range(2)]
    half = [slice(b * HALF, (b + 1) * HALF) for b in range(2)]

    loads[0].wait()
    loads[1].wait()
    for h in range(2):
        scatter(tn(v[:, cols[h]], k[:, cols[h]]), h, scat_f)
    pl.semaphore_wait(barrier, n_y - 1 + 2 * reach + n_head - 1 + 2)
    for step in range(1, n_y):
        other = lax.rem(my_y + step, n_y)
        pltpu.make_async_remote_copy(
            scat_f.at[pl.ds(other * n_z, n_z)], mid.at[my_y], leg_send.at[0], leg_recv.at[0],
            device_id={"ctx": other * n_z + my_z, "head": mine}, device_id_type=MESH,
        ).start()
    def halo_copy(i, src, dst, first, count):
        return pltpu.make_async_remote_copy(
            src.at[pl.ds(HALF + first, count)], dst.at[pl.ds(first, count)],
            halo_send.at[i], halo_recv.at[i],
            device_id={"ctx": following, "head": mine}, device_id_type=MESH,
        )

    halo_out = [
        halo_copy(0, k, k_halo, 0, HALF),
        halo_copy(1, v, v_halo, 0, HALF // 2),
        halo_copy(4, v, v_halo, HALF // 2, HALF // 2),
    ]

    mid[pl.ds(my_y, 1)] = scat_f[pl.ds(my_y * n_z, n_z)][None]

    def relay(i):
        for step in (relays[i], n_z - relays[i]):
            pl.semaphore_signal(
                known.at[i], inc=1, device_id={"ctx": at_z(step), "head": mine},
                device_id_type=MESH,
            )

    for i in range(len(relays)):
        if i:
            pl.semaphore_wait(known.at[i - 1], 2)
        relay(i)
        if i == 0:
            halo_out[0].start()
    for load in loads[2:]:
        load.wait()
    position = me * tokens + lax.broadcasted_iota(jnp.int32, (1, tokens), 1)
    coef = 1.0 / jnp.sqrt(HEAD_DIM * (position + 1).astype(F32))
    lower = lax.broadcasted_iota(jnp.int32, (HALF, HALF), 0) > lax.broadcasted_iota(
        jnp.int32, (HALF, HALF), 1
    )
    no_halo = jnp.where(me == 0, -1e30, 0.0).astype(F32)
    scaled_t[...] = (gain[...].astype(F32).reshape(1, 256) * cot[...].astype(F32)).T

    def near(b, h, own, halo):
        prev_part = halo[:, cols[h]] if b == 0 else own[half[0], cols[h]]
        return prev_part, own[half[b], cols[h]]

    def forward(b, h):
        query = q[half[b], cols[h]]
        key_prev, key_own = near(b, h, k, k_halo)
        value_prev, value_own = near(b, h, v, v_halo)
        prev = nt(key_prev, query)
        own = nt(key_own, query)
        c = coef[:, half[b]]
        logits = jnp.where(lower, prev + no_halo if b == 0 else prev, own)
        peak = jnp.max(logits, 0, keepdims=True)
        weight = jnp.exp((logits - peak) * scale)
        weight = weight * (1.0 / jnp.sum(weight, 0, keepdims=True))
        probs[h, b] = weight
        mix_own = jnp.where(lower, 0.0, weight + c * own).astype(BF16)
        mix_prev = jnp.where(lower, weight, 0.0)
        if b == 1:
            mix_prev = mix_prev + c * prev
        mix_prev = mix_prev.astype(BF16)
        w_own[h, b] = mix_own
        w_prev[h, b] = mix_prev
        local[cols[h], half[b]] = tn(value_own, mix_own) + tn(value_prev, mix_prev)

    for h in range(2):
        forward(1, h)
    whole = mid.at[pl.ds(0, n_y - 1)]
    pltpu.make_async_copy(whole, whole, leg_recv.at[0]).wait()
    if relays:
        pl.semaphore_wait(known.at[len(relays) - 1], 2)
    for step in sorted(range(1, n_z), key=lambda d: -min(d, n_z - d)):
        other = lax.rem(my_z + step, n_z)
        pltpu.make_async_remote_copy(
            mid.at[:, other], got_f.at[my_z], leg_send.at[1], leg_recv.at[1],
            device_id={"ctx": at_z(step), "head": mine}, device_id_type=MESH,
        ).start()
    halo_out[1].start()
    got_f[pl.ds(my_z, 1)] = mid[:, pl.ds(my_z, 1)].reshape(1, n_y, rows, HEAD_DIM)
    part = got_f.at[pl.ds(0, n_z - 1)]
    pltpu.make_async_copy(part, part, leg_recv.at[1]).wait()
    running(lambda i: got_f[i % n_z, i // n_z], back_f, range(n_ctx))
    exchange(back_f, pre, 0)
    halo_out[1].wait()
    halo_out[2].start()
    halo_out[0].wait()
    halo_out[2].wait()
    for h in range(2):
        forward(0, h)
    arrived(pre, 0)
    collect(pre, flat)
    prefix = flat[...].astype(BF16)

    hidden = []
    for h in range(2):
        hidden.append(local[cols[h], :] + coef * nt(prefix[cols[h], :], q[:, cols[h]]))
    squares = sum(jnp.sum(x * x, 0, keepdims=True) for x in hidden)
    crossed = sum(
        jnp.sum(x * scaled_t[cols[h], :], 0, keepdims=True) for h, x in enumerate(hidden)
    )
    stat_mine[0:1, :] = squares
    stat_mine[1:2, :] = crossed
    shares = [
        pltpu.make_async_remote_copy(
            stat_mine, stat_all.at[mine], stat_send, stat_recv,
            device_id={"ctx": me, "head": lax.rem(mine + step, n_head)}, device_id_type=MESH,
        )
        for step in range(n_head - 1, 0, -1)
    ]
    for copy in shares:
        copy.start()
    stat_all[pl.ds(mine, 1)] = stat_mine[...][None]
    for h in range(2):
        local[cols[h], :] = hidden[h]
    others = stat_all.at[pl.ds(0, n_head - 1)]
    pltpu.make_async_copy(others, others, stat_recv).wait()
    sums = stat_all[0]
    for i in range(1, n_head):
        sums = sums + stat_all[i]
    recip = 1.0 / jnp.sqrt(sums[0:1] / features + EPS)
    pull = recip * recip * recip * sums[1:2] / features

    for h in range(2):
        full = recip * scaled_t[cols[h], :] - local[cols[h], :] * pull
        grad_t[cols[h], :] = full.astype(BF16)
        grad_u = (full * coef).astype(BF16)
        gradu_t[cols[h], :] = grad_u
        scatter(nn(grad_u, q[:, cols[h]]), h, scat_b)
    exchange(scat_b, got_b, 1)

    dk_acc[...] = jnp.zeros_like(dk_acc)
    dv_acc[...] = jnp.zeros_like(dv_acc)

    def backward(b, h):
        query = q[half[b], cols[h]]
        key_prev, key_own = near(b, h, k, k_halo)
        value_prev, value_own = near(b, h, v, v_halo)
        grad = grad_t[cols[h], half[b]]
        c = coef[:, half[b]]
        prev = nn(value_prev, grad)
        own = nn(value_own, grad)
        weight = probs[h, b]
        pulled = jnp.where(lower, prev, own)
        delta = jnp.sum(weight * pulled, 0, keepdims=True)
        d_logits = weight * (pulled - delta) * scale
        d_own = jnp.where(lower, 0.0, d_logits + c * own).astype(BF16)
        d_prev = jnp.where(lower, d_logits, 0.0)
        if b == 1:
            d_prev = d_prev + c * prev
        d_prev = d_prev.astype(BF16)
        far = tn(gradu_t[cols[h], half[b]], prefix[cols[h], :])
        dq[half[b], cols[h]] = (far + tn(d_own, key_own) + tn(d_prev, key_prev)).astype(BF16)
        dk_acc[half[b], cols[h]] += nn(d_own, query)
        dv_acc[half[b], cols[h]] += nt(w_own[h, b], grad)
        if b == 0:
            dk_give[:, cols[h]] = nn(d_prev, query).astype(BF16)
            dv_give[:, cols[h]] = nt(w_prev[h, b], grad).astype(BF16)
        else:
            dk_acc[half[0], cols[h]] += nn(d_prev, query)
            dv_acc[half[0], cols[h]] += nt(w_prev[h, b], grad)

    for h in range(2):
        backward(0, h)
    halo_back = [
        pltpu.make_async_remote_copy(
            src, dst, halo_send.at[2 + i], halo_recv.at[2 + i],
            device_id={"ctx": before, "head": mine}, device_id_type=MESH,
        )
        for i, (src, dst) in enumerate(((dk_give, dk_take), (dv_give, dv_take)))
    ]
    for copy in halo_back:
        copy.start()
    for h in range(2):
        backward(1, h)

    arrived(got_b, 1)
    running(lambda i: got_b[i], back_b, range(n_ctx - 1, -1, -1))
    exchange(back_b, post, 2)

    out[...] = ((local[...] * recip).T * gain[...].astype(F32).reshape(1, 256)).astype(BF16)
    for copy in halo_back:
        copy.wait()
    dk_acc[half[1], :] += dk_take[...].astype(F32)
    dv_acc[half[1], :] += dv_take[...].astype(F32)

    arrived(post, 2)
    collect(post, flat)
    suffix[...] = flat[...].astype(BF16)
    for phase, src in enumerate((back_f, scat_b, back_b)):
        left(src, phase)
    pltpu.make_async_copy(whole, whole, leg_send.at[0]).wait()
    pltpu.make_async_copy(part, part, leg_send.at[1]).wait()
    sent = stat_all.at[pl.ds(0, n_head - 1)]
    pltpu.make_async_copy(sent, sent, stat_send).wait()


def finish(out, dq, dk_acc, dv_acc, suffix, k, v, out_hbm, dq_hbm, dk_hbm, dv_hbm, dk, dv, sem):
    stores = [
        pltpu.make_async_copy(src, dst, sem.at[i])
        for i, (src, dst) in enumerate(((out, out_hbm), (dq, dq_hbm), (dk, dk_hbm), (dv, dv_hbm)))
    ]
    stores[0].start()
    stores[1].start()
    cols = [slice(h * HEAD_DIM, (h + 1) * HEAD_DIM) for h in range(2)]
    for c in cols:
        dk[:, c] = (dk_acc[:, c] + nn(v[:, c], suffix[c, :])).astype(BF16)
    stores[2].start()
    for c in cols:
        dv[:, c] = (dv_acc[:, c] + nt(k[:, c], suffix[c, :])).astype(BF16)
    stores[3].start()
    for store in stores:
        store.wait()


def on_device(n_ctx, n_z, n_head, queries, keys, values, gain, cotangent):
    tokens, width = queries.shape
    n_y = n_ctx // n_z
    pieces = (n_ctx, 256 // n_ctx, HEAD_DIM)
    block = jax.ShapeDtypeStruct((tokens, width), BF16)
    wide = pltpu.VMEM((tokens, width), BF16)
    halo = pltpu.VMEM((HALF, width), BF16)
    piece = pltpu.VMEM(pieces, BF16)
    square = (2, 2, HALF, HALF)
    turned = (width, tokens)
    operands = (queries, keys, values, gain, cotangent)
    summed = jax.ShapeDtypeStruct((tokens, width), F32)
    vmem = pl.BlockSpec(memory_space=pltpu.VMEM)
    anywhere = pl.BlockSpec(memory_space=pl.ANY)
    results = pl.pallas_call(
        functools.partial(kernel, n_ctx, n_z, n_head),
        out_shape=[
            block, block, summed, summed, jax.ShapeDtypeStruct((width, HEAD_DIM), BF16), block,
            block,
        ],
        in_specs=[anywhere] * 5,
        out_specs=[vmem] * 7,
        scratch_shapes=[
            wide, pltpu.VMEM((width,), BF16), wide,
            halo, halo, halo, halo, halo, halo,
            piece, pltpu.VMEM((n_y, n_z, *pieces[1:]), BF16),
            pltpu.VMEM((n_z, n_y, *pieces[1:]), BF16), piece, piece, piece, piece, piece, piece,
            pltpu.VMEM((256, HEAD_DIM), F32),
            pltpu.VMEM((2, tokens), F32), pltpu.VMEM((n_head, 2, tokens), F32),
            pltpu.VMEM(square, F32), pltpu.VMEM(square, BF16), pltpu.VMEM(square, BF16),
            pltpu.VMEM(turned, F32), pltpu.VMEM(turned, F32),
            pltpu.VMEM(turned, BF16), pltpu.VMEM(turned, BF16),
            pltpu.SemaphoreType.DMA((5,)),
            pltpu.SemaphoreType.DMA((2,)), pltpu.SemaphoreType.DMA((2,)),
            pltpu.SemaphoreType.REGULAR((4,)),
            pltpu.SemaphoreType.DMA((3,)), pltpu.SemaphoreType.DMA((3,)),
            pltpu.SemaphoreType.DMA((5,)), pltpu.SemaphoreType.DMA((5,)),
            pltpu.SemaphoreType.DMA, pltpu.SemaphoreType.DMA,
        ],
        compiler_params=pltpu.CompilerParams(
            collective_id=0, has_side_effects=True, vmem_limit_bytes=48 << 20
        ),
    )(*[pltpu.with_memory_space_constraint(x, pltpu.HBM) for x in operands])
    return pl.pallas_call(
        finish,
        out_shape=[block] * 4,
        in_specs=[vmem] * 7,
        out_specs=[anywhere] * 4,
        scratch_shapes=[wide, wide, pltpu.SemaphoreType.DMA((4,))],
        compiler_params=pltpu.CompilerParams(vmem_limit_bytes=32 << 20),
    )(*[pltpu.with_memory_space_constraint(x, pltpu.VMEM) for x in results])


def solution(mesh):
    n_ctx, n_head = mesh.shape["ctx"], mesh.shape["head"]
    n_z = 16 if n_ctx % 16 == 0 else n_ctx // 2
    return jax.shard_map(
        functools.partial(on_device, n_ctx, n_z, n_head),
        mesh=mesh,
        in_specs=(
            P("ctx", "head"), P("ctx", "head"), P("ctx", "head"), P("head"), P("ctx", "head"),
        ),
        out_specs=(P("ctx", "head"),) * 4,
        check_vma=False,
    )
```

```python
import functools
import math

import jax
import jax.numpy as jnp
from jax import lax
from jax.experimental import pallas as pl
from jax.experimental.pallas import tpu as pltpu
from jax.sharding import PartitionSpec as P

HEAD_DIM = 128
WINDOW = 256
HALF = 256
EPS = 1e-06
MESH = pl.DeviceIdType.MESH
F32 = jnp.float32
BF16 = jnp.bfloat16


def dot(left, right, left_dim, right_dim):
    return lax.dot_general(
        left, right, (((left_dim,), (right_dim,)), ((), ())), preferred_element_type=F32
    )


def nn(left, right):
    return dot(left, right, 1, 0)


def nt(left, right):
    return dot(left, right, 1, 1)


def tn(left, right):
    return dot(left, right, 0, 0)


def kernel(
    n_ctx, n_z, n_head,
    q_hbm, k_hbm, v_hbm, gain_hbm, cot_hbm,
    out, dq, dk_acc, dv_acc, suffix, k, v,
    q, gain, cot,
    k_halo, v_halo, dk_give, dv_give, dk_take, dv_take,
    scat_f, mid, got_f, back_f, pre, scat_b, got_b, back_b, post, flat,
    stat_mine, stat_all,
    probs, w_own, w_prev, local, scaled_t, grad_t, gradu_t,
    in_sem, leg_send, leg_recv, known, scan_send, scan_recv, halo_send, halo_recv, stat_send, stat_recv,
):
    me = lax.axis_index("ctx")
    mine = lax.axis_index("head")
    n_y = n_ctx // n_z
    my_y = me // n_z
    my_z = lax.rem(me, n_z)
    following = lax.rem(me + 1, n_ctx)
    before = lax.rem(me + n_ctx - 1, n_ctx)
    rows = 256 // n_ctx
    tokens = 2 * HALF
    features = 256 * n_head
    scale = 1.0 / math.sqrt(HEAD_DIM)

    barrier = pltpu.get_barrier_semaphore()

    reach = max(1, n_z // 8)
    relays = []
    while reach << len(relays) < n_z // 2:
        relays.append(reach << len(relays))

    def at_z(step):
        return my_y * n_z + lax.rem(my_z + step, n_z)

    y_order = sorted(range(n_y), key=lambda d: -min(d, n_y - d))

    def farthest_first(visit):
        def at(away_y, away_z):
            visit(lax.rem(my_y + away_y, n_y) * n_z + lax.rem(my_z + away_z, n_z))

        def step(i, carry):
            away_z = n_z // 2 + ((i + 1) // 2) * (1 - 2 * lax.rem(i, 2))
            for away_y in y_order:
                at(away_y, away_z)
            return carry

        lax.fori_loop(0, n_z - 1, step, 0)
        for away_y in y_order:
            if away_y:
                at(away_y, 0)

    def greet(target, head):
        pl.semaphore_signal(
            barrier, inc=1, device_id={"ctx": target, "head": head}, device_id_type=MESH
        )

    for step in range(1, n_y):
        greet(lax.rem(my_y + step, n_y) * n_z + my_z, mine)
    for step in range(reach, 0, -1):
        greet(at_z(step), mine)
        greet(at_z(n_z - step), mine)
    for step in range(1, n_head):
        greet(me, lax.rem(mine + step, n_head))
    greet(following, mine)
    greet(before, mine)

    loads = [
        pltpu.make_async_copy(src, dst, in_sem.at[i])
        for i, (src, dst) in enumerate(
            ((k_hbm, k), (v_hbm, v), (q_hbm, q), (cot_hbm, cot), (gain_hbm, gain))
        )
    ]
    for load in loads:
        load.start()

    def exchange(src, dst, phase):
        def send(target):
            pltpu.make_async_remote_copy(
                src.at[target], dst.at[me], scan_send.at[phase], scan_recv.at[phase],
                device_id={"ctx": target, "head": mine}, device_id_type=MESH,
            ).start()

        farthest_first(send)
        dst[pl.ds(me, 1)] = src[pl.ds(me, 1)]

    def arrived(dst, phase):
        part = dst.at[pl.ds(0, n_ctx - 1)]
        pltpu.make_async_copy(part, part, scan_recv.at[phase]).wait()

    def left(src, phase):
        part = src.at[pl.ds(0, n_ctx - 1)]
        pltpu.make_async_copy(part, part, scan_send.at[phase]).wait()

    def scatter(state, head, dst):
        for i in range(HEAD_DIM // rows):
            dst[head * (HEAD_DIM // rows) + i] = state[i * rows : (i + 1) * rows].astype(BF16)

    def running(src, dst, order):
        total = jnp.zeros((rows, HEAD_DIM), F32)
        for i in order:
            dst[i] = total.astype(BF16)
            total = total + src(i).astype(F32)

    def collect(src, dst):
        for i in range(n_ctx):
            dst[i * rows : (i + 1) * rows, :] = src[i].astype(F32)

    cols = [slice(h * HEAD_DIM, (h + 1) * HEAD_DIM) for h in range(2)]
    half = [slice(b * HALF, (b + 1) * HALF) for b in range(2)]

    loads[0].wait()
    loads[1].wait()
    for h in range(2):
        scatter(tn(v[:, cols[h]], k[:, cols[h]]), h, scat_f)
    pl.semaphore_wait(barrier, n_y - 1 + 2 * reach + n_head - 1 + 2)
    for step in range(1, n_y):
        other = lax.rem(my_y + step, n_y)
        pltpu.make_async_remote_copy(
            scat_f.at[pl.ds(other * n_z, n_z)], mid.at[my_y], leg_send.at[0], leg_recv.at[0],
            device_id={"ctx": other * n_z + my_z, "head": mine}, device_id_type=MESH,
        ).start()
    def halo_copy(i, src, dst, first, count):
        return pltpu.make_async_remote_copy(
            src.at[pl.ds(HALF + first, count)], dst.at[pl.ds(first, count)],
            halo_send.at[i], halo_recv.at[i],
            device_id={"ctx": following, "head": mine}, device_id_type=MESH,
        )

    halo_out = [
        halo_copy(0, k, k_halo, 0, HALF),
        halo_copy(1, v, v_halo, 0, HALF // 2),
        halo_copy(4, v, v_halo, HALF // 2, HALF // 2),
    ]

    mid[pl.ds(my_y, 1)] = scat_f[pl.ds(my_y * n_z, n_z)][None]

    def relay(i):
        for step in (relays[i], n_z - relays[i]):
            pl.semaphore_signal(
                known.at[i], inc=1, device_id={"ctx": at_z(step), "head": mine},
                device_id_type=MESH,
            )

    for i in range(len(relays)):
        if i:
            pl.semaphore_wait(known.at[i - 1], 2)
        relay(i)
        if i == 0:
            halo_out[0].start()
    for load in loads[2:]:
        load.wait()
    position = me * tokens + lax.broadcasted_iota(jnp.int32, (1, tokens), 1)
    coef = 1.0 / jnp.sqrt(HEAD_DIM * (position + 1).astype(F32))
    lower = lax.broadcasted_iota(jnp.int32, (HALF, HALF), 0) > lax.broadcasted_iota(
        jnp.int32, (HALF, HALF), 1
    )
    no_halo = jnp.where(me == 0, -1e30, 0.0).astype(F32)
    scaled_t[...] = (gain[...].astype(F32).reshape(1, 256) * cot[...].astype(F32)).T

    def near(b, h, own, halo):
        prev_part = halo[:, cols[h]] if b == 0 else own[half[0], cols[h]]
        return prev_part, own[half[b], cols[h]]

    def forward(b, h):
        query = q[half[b], cols[h]]
        key_prev, key_own = near(b, h, k, k_halo)
        value_prev, value_own = near(b, h, v, v_halo)
        prev = nt(key_prev, query)
        own = nt(key_own, query)
        c = coef[:, half[b]]
        logits = jnp.where(lower, prev + no_halo if b == 0 else prev, own)
        peak = jnp.max(logits, 0, keepdims=True)
        weight = jnp.exp((logits - peak) * scale)
        weight = weight * (1.0 / jnp.sum(weight, 0, keepdims=True))
        probs[h, b] = weight
        mix_own = jnp.where(lower, 0.0, weight + c * own).astype(BF16)
        mix_prev = jnp.where(lower, weight, 0.0)
        if b == 1:
            mix_prev = mix_prev + c * prev
        mix_prev = mix_prev.astype(BF16)
        w_own[h, b] = mix_own
        w_prev[h, b] = mix_prev
        local[cols[h], half[b]] = tn(value_own, mix_own) + tn(value_prev, mix_prev)

    for h in range(2):
        forward(1, h)
    whole = mid.at[pl.ds(0, n_y - 1)]
    pltpu.make_async_copy(whole, whole, leg_recv.at[0]).wait()
    if relays:
        pl.semaphore_wait(known.at[len(relays) - 1], 2)
    for step in sorted(range(1, n_z), key=lambda d: -min(d, n_z - d)):
        other = lax.rem(my_z + step, n_z)
        pltpu.make_async_remote_copy(
            mid.at[:, other], got_f.at[my_z], leg_send.at[1], leg_recv.at[1],
            device_id={"ctx": at_z(step), "head": mine}, device_id_type=MESH,
        ).start()
    halo_out[1].start()
    got_f[pl.ds(my_z, 1)] = mid[:, pl.ds(my_z, 1)].reshape(1, n_y, rows, HEAD_DIM)
    part = got_f.at[pl.ds(0, n_z - 1)]
    pltpu.make_async_copy(part, part, leg_recv.at[1]).wait()
    running(lambda i: got_f[i % n_z, i // n_z], back_f, range(n_ctx))
    exchange(back_f, pre, 0)
    halo_out[1].wait()
    halo_out[2].start()
    halo_out[0].wait()
    halo_out[2].wait()
    for h in range(2):
        forward(0, h)
    arrived(pre, 0)
    collect(pre, flat)
    prefix = flat[...].astype(BF16)

    hidden = []
    for h in range(2):
        hidden.append(local[cols[h], :] + coef * nt(prefix[cols[h], :], q[:, cols[h]]))
    squares = sum(jnp.sum(x * x, 0, keepdims=True) for x in hidden)
    crossed = sum(
        jnp.sum(x * scaled_t[cols[h], :], 0, keepdims=True) for h, x in enumerate(hidden)
    )
    stat_mine[0:1, :] = squares
    stat_mine[1:2, :] = crossed
    shares = [
        pltpu.make_async_remote_copy(
            stat_mine, stat_all.at[mine], stat_send, stat_recv,
            device_id={"ctx": me, "head": lax.rem(mine + step, n_head)}, device_id_type=MESH,
        )
        for step in range(n_head - 1, 0, -1)
    ]
    for copy in shares:
        copy.start()
    stat_all[pl.ds(mine, 1)] = stat_mine[...][None]
    for h in range(2):
        local[cols[h], :] = hidden[h]
    others = stat_all.at[pl.ds(0, n_head - 1)]
    pltpu.make_async_copy(others, others, stat_recv).wait()
    sums = stat_all[0]
    for i in range(1, n_head):
        sums = sums + stat_all[i]
    recip = 1.0 / jnp.sqrt(sums[0:1] / features + EPS)
    pull = recip * recip * recip * sums[1:2] / features

    for h in range(2):
        full = recip * scaled_t[cols[h], :] - local[cols[h], :] * pull
        grad_t[cols[h], :] = full.astype(BF16)
        grad_u = (full * coef).astype(BF16)
        gradu_t[cols[h], :] = grad_u
        scatter(nn(grad_u, q[:, cols[h]]), h, scat_b)
    exchange(scat_b, got_b, 1)

    dk_acc[...] = jnp.zeros_like(dk_acc)
    dv_acc[...] = jnp.zeros_like(dv_acc)

    def backward(b, h):
        query = q[half[b], cols[h]]
        key_prev, key_own = near(b, h, k, k_halo)
        value_prev, value_own = near(b, h, v, v_halo)
        grad = grad_t[cols[h], half[b]]
        c = coef[:, half[b]]
        prev = nn(value_prev, grad)
        own = nn(value_own, grad)
        weight = probs[h, b]
        pulled = jnp.where(lower, prev, own)
        delta = jnp.sum(weight * pulled, 0, keepdims=True)
        d_logits = weight * (pulled - delta) * scale
        d_own = jnp.where(lower, 0.0, d_logits + c * own).astype(BF16)
        d_prev = jnp.where(lower, d_logits, 0.0)
        if b == 1:
            d_prev = d_prev + c * prev
        d_prev = d_prev.astype(BF16)
        far = tn(gradu_t[cols[h], half[b]], prefix[cols[h], :])
        dq[half[b], cols[h]] = (far + tn(d_own, key_own) + tn(d_prev, key_prev)).astype(BF16)
        dk_acc[half[b], cols[h]] += nn(d_own, query)
        dv_acc[half[b], cols[h]] += nt(w_own[h, b], grad)
        if b == 0:
            dk_give[:, cols[h]] = nn(d_prev, query).astype(BF16)
            dv_give[:, cols[h]] = nt(w_prev[h, b], grad).astype(BF16)
        else:
            dk_acc[half[0], cols[h]] += nn(d_prev, query)
            dv_acc[half[0], cols[h]] += nt(w_prev[h, b], grad)

    for h in range(2):
        backward(0, h)
    halo_back = [
        pltpu.make_async_remote_copy(
            src, dst, halo_send.at[2 + i], halo_recv.at[2 + i],
            device_id={"ctx": before, "head": mine}, device_id_type=MESH,
        )
        for i, (src, dst) in enumerate(((dk_give, dk_take), (dv_give, dv_take)))
    ]
    halo_back[0].start()
    for h in range(2):
        backward(1, h)

    arrived(got_b, 1)
    running(lambda i: got_b[i], back_b, range(n_ctx - 1, -1, -1))
    exchange(back_b, post, 2)
    halo_back[1].start()

    out[...] = ((local[...] * recip).T * gain[...].astype(F32).reshape(1, 256)).astype(BF16)
    for copy in halo_back:
        copy.wait()
    dk_acc[half[1], :] += dk_take[...].astype(F32)
    dv_acc[half[1], :] += dv_take[...].astype(F32)

    arrived(post, 2)
    collect(post, flat)
    suffix[...] = flat[...].astype(BF16)
    for phase, src in enumerate((back_f, scat_b, back_b)):
        left(src, phase)
    pltpu.make_async_copy(whole, whole, leg_send.at[0]).wait()
    pltpu.make_async_copy(part, part, leg_send.at[1]).wait()
    sent = stat_all.at[pl.ds(0, n_head - 1)]
    pltpu.make_async_copy(sent, sent, stat_send).wait()


def finish(out, dq, dk_acc, dv_acc, suffix, k, v, out_hbm, dq_hbm, dk_hbm, dv_hbm, dk, dv, sem):
    cols = [slice(h * HEAD_DIM, (h + 1) * HEAD_DIM) for h in range(2)]
    stores = [
        pltpu.make_async_copy(out, out_hbm, sem.at[0]), pltpu.make_async_copy(dq, dq_hbm, sem.at[1])
    ]
    for store in stores:
        store.start()

    def hand_on(src, dst, first, i):
        part = pl.ds(first, HALF)
        store = pltpu.make_async_copy(src.at[part], dst.at[part], sem.at[i])
        store.start()
        stores.append(store)

    for b in range(2):
        half = slice(b * HALF, (b + 1) * HALF)
        for c in cols:
            dk[half, c] = (dk_acc[half, c] + nn(v[half, c], suffix[c, :])).astype(BF16)
        hand_on(dk, dk_hbm, b * HALF, 2 + 2 * b)
        for c in cols:
            dv[half, c] = (dv_acc[half, c] + nt(k[half, c], suffix[c, :])).astype(BF16)
        hand_on(dv, dv_hbm, b * HALF, 3 + 2 * b)
    for store in stores:
        store.wait()


def on_device(n_ctx, n_z, n_head, queries, keys, values, gain, cotangent):
    tokens, width = queries.shape
    n_y = n_ctx // n_z
    pieces = (n_ctx, 256 // n_ctx, HEAD_DIM)
    block = jax.ShapeDtypeStruct((tokens, width), BF16)
    wide = pltpu.VMEM((tokens, width), BF16)
    halo = pltpu.VMEM((HALF, width), BF16)
    piece = pltpu.VMEM(pieces, BF16)
    square = (2, 2, HALF, HALF)
    turned = (width, tokens)
    operands = (queries, keys, values, gain, cotangent)
    summed = jax.ShapeDtypeStruct((tokens, width), F32)
    vmem = pl.BlockSpec(memory_space=pltpu.VMEM)
    anywhere = pl.BlockSpec(memory_space=pl.ANY)
    results = pl.pallas_call(
        functools.partial(kernel, n_ctx, n_z, n_head),
        out_shape=[
            block, block, summed, summed, jax.ShapeDtypeStruct((width, HEAD_DIM), BF16), block,
            block,
        ],
        in_specs=[anywhere] * 5,
        out_specs=[vmem] * 7,
        scratch_shapes=[
            wide, pltpu.VMEM((width,), BF16), wide,
            halo, halo, halo, halo, halo, halo,
            piece, pltpu.VMEM((n_y, n_z, *pieces[1:]), BF16),
            pltpu.VMEM((n_z, n_y, *pieces[1:]), BF16), piece, piece, piece, piece, piece, piece,
            pltpu.VMEM((256, HEAD_DIM), F32),
            pltpu.VMEM((2, tokens), F32), pltpu.VMEM((n_head, 2, tokens), F32),
            pltpu.VMEM(square, F32), pltpu.VMEM(square, BF16), pltpu.VMEM(square, BF16),
            pltpu.VMEM(turned, F32), pltpu.VMEM(turned, F32),
            pltpu.VMEM(turned, BF16), pltpu.VMEM(turned, BF16),
            pltpu.SemaphoreType.DMA((5,)),
            pltpu.SemaphoreType.DMA((2,)), pltpu.SemaphoreType.DMA((2,)),
            pltpu.SemaphoreType.REGULAR((4,)),
            pltpu.SemaphoreType.DMA((3,)), pltpu.SemaphoreType.DMA((3,)),
            pltpu.SemaphoreType.DMA((5,)), pltpu.SemaphoreType.DMA((5,)),
            pltpu.SemaphoreType.DMA, pltpu.SemaphoreType.DMA,
        ],
        compiler_params=pltpu.CompilerParams(
            collective_id=0, has_side_effects=True, vmem_limit_bytes=48 << 20
        ),
    )(*[pltpu.with_memory_space_constraint(x, pltpu.HBM) for x in operands])
    return pl.pallas_call(
        finish,
        out_shape=[block] * 4,
        in_specs=[vmem] * 7,
        out_specs=[anywhere] * 4,
        scratch_shapes=[wide, wide, pltpu.SemaphoreType.DMA((6,))],
        compiler_params=pltpu.CompilerParams(vmem_limit_bytes=32 << 20),
    )(*[pltpu.with_memory_space_constraint(x, pltpu.VMEM) for x in results])


def solution(mesh):
    n_ctx, n_head = mesh.shape["ctx"], mesh.shape["head"]
    n_z = 16 if n_ctx % 16 == 0 else n_ctx // 2
    return jax.shard_map(
        functools.partial(on_device, n_ctx, n_z, n_head),
        mesh=mesh,
        in_specs=(
            P("ctx", "head"), P("ctx", "head"), P("ctx", "head"), P("head"), P("ctx", "head"),
        ),
        out_specs=(P("ctx", "head"),) * 4,
        check_vma=False,
    )
```

```python
import functools
import math

import jax
import jax.numpy as jnp
from jax import lax
from jax.experimental import pallas as pl
from jax.experimental.pallas import tpu as pltpu
from jax.sharding import PartitionSpec as P

HEAD_DIM = 128
WINDOW = 256
HALF = 256
EPS = 1e-06
MESH = pl.DeviceIdType.MESH
F32 = jnp.float32
BF16 = jnp.bfloat16


def dot(left, right, left_dim, right_dim):
    return lax.dot_general(
        left, right, (((left_dim,), (right_dim,)), ((), ())), preferred_element_type=F32
    )


def nn(left, right):
    return dot(left, right, 1, 0)


def nt(left, right):
    return dot(left, right, 1, 1)


def tn(left, right):
    return dot(left, right, 0, 0)


def kernel(
    n_ctx, n_z, n_head,
    q_hbm, k_hbm, v_hbm, gain_hbm, cot_hbm,
    out, dq, dk_acc, dv_acc, suffix, k, v,
    q, gain, cot,
    k_halo, v_halo, dk_give, dv_give, dk_take, dv_take,
    scat_f, mid, got_f, back_f, pre, scat_b, got_b, back_b, post, flat,
    stat_mine, stat_all,
    probs, w_own, w_prev, local, scaled_t, grad_t, gradu_t,
    in_sem, leg_send, leg_recv, known, scan_send, scan_recv, halo_send, halo_recv, stat_send, stat_recv,
):
    me = lax.axis_index("ctx")
    mine = lax.axis_index("head")
    n_y = n_ctx // n_z
    my_y = me // n_z
    my_z = lax.rem(me, n_z)
    following = lax.rem(me + 1, n_ctx)
    before = lax.rem(me + n_ctx - 1, n_ctx)
    rows = 256 // n_ctx
    tokens = 2 * HALF
    features = 256 * n_head
    scale = 1.0 / math.sqrt(HEAD_DIM)

    barrier = pltpu.get_barrier_semaphore()

    reach = max(1, n_z // 8)
    relays = []
    while reach << len(relays) < n_z // 2:
        relays.append(reach << len(relays))

    def at_z(step):
        return my_y * n_z + lax.rem(my_z + step, n_z)

    y_order = sorted(range(n_y), key=lambda d: -min(d, n_y - d))

    def farthest_first(visit):
        def at(away_y, away_z):
            visit(lax.rem(my_y + away_y, n_y) * n_z + lax.rem(my_z + away_z, n_z))

        def step(i, carry):
            away_z = n_z // 2 + ((i + 1) // 2) * (1 - 2 * lax.rem(i, 2))
            for away_y in y_order:
                at(away_y, away_z)
            return carry

        lax.fori_loop(0, n_z - 1, step, 0)
        for away_y in y_order:
            if away_y:
                at(away_y, 0)

    def greet(target, head):
        pl.semaphore_signal(
            barrier, inc=1, device_id={"ctx": target, "head": head}, device_id_type=MESH
        )

    for step in range(1, n_y):
        greet(lax.rem(my_y + step, n_y) * n_z + my_z, mine)
    for step in range(reach, 0, -1):
        greet(at_z(step), mine)
        greet(at_z(n_z - step), mine)
    for step in range(1, n_head):
        greet(me, lax.rem(mine + step, n_head))
    greet(following, mine)
    greet(before, mine)

    loads = [
        pltpu.make_async_copy(src, dst, in_sem.at[i])
        for i, (src, dst) in enumerate(
            ((k_hbm, k), (v_hbm, v), (q_hbm, q), (cot_hbm, cot), (gain_hbm, gain))
        )
    ]
    for load in loads:
        load.start()

    def exchange(src, dst, phase):
        def send(target):
            pltpu.make_async_remote_copy(
                src.at[target], dst.at[me], scan_send.at[phase], scan_recv.at[phase],
                device_id={"ctx": target, "head": mine}, device_id_type=MESH,
            ).start()

        farthest_first(send)
        dst[pl.ds(me, 1)] = src[pl.ds(me, 1)]

    def arrived(dst, phase):
        part = dst.at[pl.ds(0, n_ctx - 1)]
        pltpu.make_async_copy(part, part, scan_recv.at[phase]).wait()

    def left(src, phase):
        part = src.at[pl.ds(0, n_ctx - 1)]
        pltpu.make_async_copy(part, part, scan_send.at[phase]).wait()

    def scatter(state, head, dst):
        for i in range(HEAD_DIM // rows):
            dst[head * (HEAD_DIM // rows) + i] = state[i * rows : (i + 1) * rows].astype(BF16)

    def running(src, dst, order):
        total = jnp.zeros((rows, HEAD_DIM), F32)
        for i in order:
            dst[i] = total.astype(BF16)
            total = total + src(i).astype(F32)

    def collect(src, dst):
        for i in range(n_ctx):
            dst[i * rows : (i + 1) * rows, :] = src[i].astype(F32)

    cols = [slice(h * HEAD_DIM, (h + 1) * HEAD_DIM) for h in range(2)]
    half = [slice(b * HALF, (b + 1) * HALF) for b in range(2)]

    loads[0].wait()
    loads[1].wait()
    for h in range(2):
        scatter(tn(v[:, cols[h]], k[:, cols[h]]), h, scat_f)
    pl.semaphore_wait(barrier, n_y - 1 + 2 * reach + n_head - 1 + 2)
    for step in range(1, n_y):
        other = lax.rem(my_y + step, n_y)
        pltpu.make_async_remote_copy(
            scat_f.at[pl.ds(other * n_z, n_z)], mid.at[my_y], leg_send.at[0], leg_recv.at[0],
            device_id={"ctx": other * n_z + my_z, "head": mine}, device_id_type=MESH,
        ).start()
    def halo_copy(i, src, dst, first, count):
        return pltpu.make_async_remote_copy(
            src.at[pl.ds(HALF + first, count)], dst.at[pl.ds(first, count)],
            halo_send.at[i], halo_recv.at[i],
            device_id={"ctx": following, "head": mine}, device_id_type=MESH,
        )

    halo_out = [
        halo_copy(0, k, k_halo, 0, HALF),
        halo_copy(1, v, v_halo, 0, HALF // 2),
        halo_copy(4, v, v_halo, HALF // 2, HALF // 2),
    ]

    mid[pl.ds(my_y, 1)] = scat_f[pl.ds(my_y * n_z, n_z)][None]

    def relay(i):
        for step in (relays[i], n_z - relays[i]):
            pl.semaphore_signal(
                known.at[i], inc=1, device_id={"ctx": at_z(step), "head": mine},
                device_id_type=MESH,
            )

    for i in range(len(relays)):
        if i:
            pl.semaphore_wait(known.at[i - 1], 2)
        relay(i)
        if i == 0:
            halo_out[0].start()
    for load in loads[2:]:
        load.wait()
    position = me * tokens + lax.broadcasted_iota(jnp.int32, (1, tokens), 1)
    coef = 1.0 / jnp.sqrt(HEAD_DIM * (position + 1).astype(F32))
    lower = lax.broadcasted_iota(jnp.int32, (HALF, HALF), 0) > lax.broadcasted_iota(
        jnp.int32, (HALF, HALF), 1
    )
    no_halo = jnp.where(me == 0, -1e30, 0.0).astype(F32)
    scaled_t[...] = (gain[...].astype(F32).reshape(1, 256) * cot[...].astype(F32)).T

    def near(b, h, own, halo):
        prev_part = halo[:, cols[h]] if b == 0 else own[half[0], cols[h]]
        return prev_part, own[half[b], cols[h]]

    def forward(b, h):
        query = q[half[b], cols[h]]
        key_prev, key_own = near(b, h, k, k_halo)
        value_prev, value_own = near(b, h, v, v_halo)
        prev = nt(key_prev, query)
        own = nt(key_own, query)
        c = coef[:, half[b]]
        logits = jnp.where(lower, prev + no_halo if b == 0 else prev, own)
        peak = jnp.max(logits, 0, keepdims=True)
        weight = jnp.exp((logits - peak) * scale)
        weight = weight * (1.0 / jnp.sum(weight, 0, keepdims=True))
        probs[h, b] = weight
        mix_own = jnp.where(lower, 0.0, weight + c * own).astype(BF16)
        mix_prev = jnp.where(lower, weight, 0.0)
        if b == 1:
            mix_prev = mix_prev + c * prev
        mix_prev = mix_prev.astype(BF16)
        w_own[h, b] = mix_own
        w_prev[h, b] = mix_prev
        local[cols[h], half[b]] = tn(value_own, mix_own) + tn(value_prev, mix_prev)

    for h in range(2):
        forward(1, h)
    whole = mid.at[pl.ds(0, n_y - 1)]
    pltpu.make_async_copy(whole, whole, leg_recv.at[0]).wait()
    if relays:
        pl.semaphore_wait(known.at[len(relays) - 1], 2)
    for step in sorted(range(1, n_z), key=lambda d: -min(d, n_z - d)):
        other = lax.rem(my_z + step, n_z)
        pltpu.make_async_remote_copy(
            mid.at[:, other], got_f.at[my_z], leg_send.at[1], leg_recv.at[1],
            device_id={"ctx": at_z(step), "head": mine}, device_id_type=MESH,
        ).start()
    halo_out[1].start()
    got_f[pl.ds(my_z, 1)] = mid[:, pl.ds(my_z, 1)].reshape(1, n_y, rows, HEAD_DIM)
    part = got_f.at[pl.ds(0, n_z - 1)]
    pltpu.make_async_copy(part, part, leg_recv.at[1]).wait()
    running(lambda i: got_f[i % n_z, i // n_z], back_f, range(n_ctx))
    exchange(back_f, pre, 0)
    halo_out[1].wait()
    halo_out[2].start()
    halo_out[0].wait()
    halo_out[2].wait()
    for h in range(2):
        forward(0, h)
    arrived(pre, 0)
    collect(pre, flat)
    prefix = flat[...].astype(BF16)

    hidden = []
    for h in range(2):
        hidden.append(local[cols[h], :] + coef * nt(prefix[cols[h], :], q[:, cols[h]]))
    squares = sum(jnp.sum(x * x, 0, keepdims=True) for x in hidden)
    crossed = sum(
        jnp.sum(x * scaled_t[cols[h], :], 0, keepdims=True) for h, x in enumerate(hidden)
    )
    stat_mine[0:1, :] = squares
    stat_mine[1:2, :] = crossed
    shares = [
        pltpu.make_async_remote_copy(
            stat_mine, stat_all.at[mine], stat_send, stat_recv,
            device_id={"ctx": me, "head": lax.rem(mine + step, n_head)}, device_id_type=MESH,
        )
        for step in sorted(range(1, n_head), key=lambda d: -min(d, n_head - d))
    ]
    for copy in shares:
        copy.start()
    stat_all[pl.ds(mine, 1)] = stat_mine[...][None]
    for h in range(2):
        local[cols[h], :] = hidden[h]
    others = stat_all.at[pl.ds(0, n_head - 1)]
    pltpu.make_async_copy(others, others, stat_recv).wait()
    sums = stat_all[0]
    for i in range(1, n_head):
        sums = sums + stat_all[i]
    recip = 1.0 / jnp.sqrt(sums[0:1] / features + EPS)
    pull = recip * recip * recip * sums[1:2] / features

    for h in range(2):
        full = recip * scaled_t[cols[h], :] - local[cols[h], :] * pull
        grad_t[cols[h], :] = full.astype(BF16)
        grad_u = (full * coef).astype(BF16)
        gradu_t[cols[h], :] = grad_u
        scatter(nn(grad_u, q[:, cols[h]]), h, scat_b)
    exchange(scat_b, got_b, 1)

    dk_acc[...] = jnp.zeros_like(dk_acc)
    dv_acc[...] = jnp.zeros_like(dv_acc)

    def backward(b, h):
        query = q[half[b], cols[h]]
        key_prev, key_own = near(b, h, k, k_halo)
        value_prev, value_own = near(b, h, v, v_halo)
        grad = grad_t[cols[h], half[b]]
        c = coef[:, half[b]]
        prev = nn(value_prev, grad)
        own = nn(value_own, grad)
        weight = probs[h, b]
        pulled = jnp.where(lower, prev, own)
        delta = jnp.sum(weight * pulled, 0, keepdims=True)
        d_logits = weight * (pulled - delta) * scale
        d_own = jnp.where(lower, 0.0, d_logits + c * own).astype(BF16)
        d_prev = jnp.where(lower, d_logits, 0.0)
        if b == 1:
            d_prev = d_prev + c * prev
        d_prev = d_prev.astype(BF16)
        far = tn(gradu_t[cols[h], half[b]], prefix[cols[h], :])
        dq[half[b], cols[h]] = (far + tn(d_own, key_own) + tn(d_prev, key_prev)).astype(BF16)
        dk_acc[half[b], cols[h]] += nn(d_own, query)
        dv_acc[half[b], cols[h]] += nt(w_own[h, b], grad)
        if b == 0:
            dk_give[:, cols[h]] = nn(d_prev, query).astype(BF16)
            dv_give[:, cols[h]] = nt(w_prev[h, b], grad).astype(BF16)
        else:
            dk_acc[half[0], cols[h]] += nn(d_prev, query)
            dv_acc[half[0], cols[h]] += nt(w_prev[h, b], grad)

    for h in range(2):
        backward(0, h)
    halo_back = [
        pltpu.make_async_remote_copy(
            src, dst, halo_send.at[2 + i], halo_recv.at[2 + i],
            device_id={"ctx": before, "head": mine}, device_id_type=MESH,
        )
        for i, (src, dst) in enumerate(((dk_give, dk_take), (dv_give, dv_take)))
    ]
    halo_back[0].start()
    for h in range(2):
        backward(1, h)

    arrived(got_b, 1)
    running(lambda i: got_b[i], back_b, range(n_ctx - 1, -1, -1))
    exchange(back_b, post, 2)
    halo_back[1].start()

    out[...] = ((local[...] * recip).T * gain[...].astype(F32).reshape(1, 256)).astype(BF16)
    for copy in halo_back:
        copy.wait()
    dk_acc[half[1], :] += dk_take[...].astype(F32)
    dv_acc[half[1], :] += dv_take[...].astype(F32)

    arrived(post, 2)
    collect(post, flat)
    suffix[...] = flat[...].astype(BF16)
    for phase, src in enumerate((back_f, scat_b, back_b)):
        left(src, phase)
    pltpu.make_async_copy(whole, whole, leg_send.at[0]).wait()
    pltpu.make_async_copy(part, part, leg_send.at[1]).wait()
    sent = stat_all.at[pl.ds(0, n_head - 1)]
    pltpu.make_async_copy(sent, sent, stat_send).wait()


def finish(out, dq, dk_acc, dv_acc, suffix, k, v, out_hbm, dq_hbm, dk_hbm, dv_hbm, dk, dv, sem):
    cols = [slice(h * HEAD_DIM, (h + 1) * HEAD_DIM) for h in range(2)]
    stores = [
        pltpu.make_async_copy(out, out_hbm, sem.at[0]), pltpu.make_async_copy(dq, dq_hbm, sem.at[1])
    ]
    for store in stores:
        store.start()

    def hand_on(src, dst, first, i):
        part = pl.ds(first, HALF)
        store = pltpu.make_async_copy(src.at[part], dst.at[part], sem.at[i])
        store.start()
        stores.append(store)

    for b in range(2):
        half = slice(b * HALF, (b + 1) * HALF)
        for c in cols:
            dk[half, c] = (dk_acc[half, c] + nn(v[half, c], suffix[c, :])).astype(BF16)
        hand_on(dk, dk_hbm, b * HALF, 2 + 2 * b)
        for c in cols:
            dv[half, c] = (dv_acc[half, c] + nt(k[half, c], suffix[c, :])).astype(BF16)
        hand_on(dv, dv_hbm, b * HALF, 3 + 2 * b)
    for store in stores:
        store.wait()


def on_device(n_ctx, n_z, n_head, queries, keys, values, gain, cotangent):
    tokens, width = queries.shape
    n_y = n_ctx // n_z
    pieces = (n_ctx, 256 // n_ctx, HEAD_DIM)
    block = jax.ShapeDtypeStruct((tokens, width), BF16)
    wide = pltpu.VMEM((tokens, width), BF16)
    halo = pltpu.VMEM((HALF, width), BF16)
    piece = pltpu.VMEM(pieces, BF16)
    square = (2, 2, HALF, HALF)
    turned = (width, tokens)
    operands = (queries, keys, values, gain, cotangent)
    summed = jax.ShapeDtypeStruct((tokens, width), F32)
    vmem = pl.BlockSpec(memory_space=pltpu.VMEM)
    anywhere = pl.BlockSpec(memory_space=pl.ANY)
    results = pl.pallas_call(
        functools.partial(kernel, n_ctx, n_z, n_head),
        out_shape=[
            block, block, summed, summed, jax.ShapeDtypeStruct((width, HEAD_DIM), BF16), block,
            block,
        ],
        in_specs=[anywhere] * 5,
        out_specs=[vmem] * 7,
        scratch_shapes=[
            wide, pltpu.VMEM((width,), BF16), wide,
            halo, halo, halo, halo, halo, halo,
            piece, pltpu.VMEM((n_y, n_z, *pieces[1:]), BF16),
            pltpu.VMEM((n_z, n_y, *pieces[1:]), BF16), piece, piece, piece, piece, piece, piece,
            pltpu.VMEM((256, HEAD_DIM), F32),
            pltpu.VMEM((2, tokens), F32), pltpu.VMEM((n_head, 2, tokens), F32),
            pltpu.VMEM(square, F32), pltpu.VMEM(square, BF16), pltpu.VMEM(square, BF16),
            pltpu.VMEM(turned, F32), pltpu.VMEM(turned, F32),
            pltpu.VMEM(turned, BF16), pltpu.VMEM(turned, BF16),
            pltpu.SemaphoreType.DMA((5,)),
            pltpu.SemaphoreType.DMA((2,)), pltpu.SemaphoreType.DMA((2,)),
            pltpu.SemaphoreType.REGULAR((4,)),
            pltpu.SemaphoreType.DMA((3,)), pltpu.SemaphoreType.DMA((3,)),
            pltpu.SemaphoreType.DMA((5,)), pltpu.SemaphoreType.DMA((5,)),
            pltpu.SemaphoreType.DMA, pltpu.SemaphoreType.DMA,
        ],
        compiler_params=pltpu.CompilerParams(
            collective_id=0, has_side_effects=True, vmem_limit_bytes=48 << 20
        ),
    )(*[pltpu.with_memory_space_constraint(x, pltpu.HBM) for x in operands])
    return pl.pallas_call(
        finish,
        out_shape=[block] * 4,
        in_specs=[vmem] * 7,
        out_specs=[anywhere] * 4,
        scratch_shapes=[wide, wide, pltpu.SemaphoreType.DMA((6,))],
        compiler_params=pltpu.CompilerParams(vmem_limit_bytes=32 << 20),
    )(*[pltpu.with_memory_space_constraint(x, pltpu.VMEM) for x in results])


def solution(mesh):
    n_ctx, n_head = mesh.shape["ctx"], mesh.shape["head"]
    n_z = 16 if n_ctx % 16 == 0 else n_ctx // 2
    return jax.shard_map(
        functools.partial(on_device, n_ctx, n_z, n_head),
        mesh=mesh,
        in_specs=(
            P("ctx", "head"), P("ctx", "head"), P("ctx", "head"), P("head"), P("ctx", "head"),
        ),
        out_specs=(P("ctx", "head"),) * 4,
        check_vma=False,
    )
```
